32 devices in a mesh: pano: 2 (over y), blk: 8 (over z, x), rows: 2 (over core).
Axes of the slice: x: 2, y: 2, z: 4, core: 2. Of those that a mesh axis runs over, the one named last changes fastest.
Arguments:
- latent: float32 [16, 256, 640], P(('pano', 'rows'), 'blk'), parts along dimension 0, may hold values from -6 to 6
- offset: int32 [2], P('pano'), parts along dimension 0, may hold values from 0 to 31
- counts: int32 [16, 64], P(('pano', 'blk')), parts along dimension 0, may hold values from 1 to 4
- conv_one: bfloat16 [3, 3, 640, 640], P(None, None, None, 'rows'), may hold values from -0.078125 to 0.078125
- conv_two: bfloat16 [3, 3, 640, 640], P(None, None, None, 'rows'), may hold values from -0.078125 to 0.078125
- gain_one: float32 [640], replicated, may hold values from 0.1 to 1.9
- gain_two: float32 [640], replicated, may hold values from 0.1 to 1.9
- time_bias: float32 [640], replicated, may hold values from -6 to 6
Outputs:
- new_latent: float32 [16, 256, 640], P(('pano', 'rows'), 'blk'), parts along dimension 0
The draws below stay inside these ranges and needn't reach their ends.
There are 2 independent parts, one for each index of `pano`. The reference program is written for one: setup_inputs(seed, part) draws one part's arguments, and reference() takes and returns one part's arrays. A program takes and returns all parts, laid end to end along the dimension named above; an argument that names none is the same for every part. Nothing has to cross between parts.
All inputs are finite; a program needn't handle non-finite values.
Results may differ from the reference program's by a relative error of at most 0.0014.
Values may be sent and summed in bfloat16 or wider, within the bound.
No kernel may reach another device: no remote copies, remote signals or barrier semaphores. Data moves between devices by JAX's collectives and lax.ppermute only.
A program may use at most 64 MiB of HBM per device.

```python
import math
import jax
import jax.numpy as jnp
from jax import lax

C = 640
GROUPS = 32
STRIDE = 32
HEIGHT = 8
WINDOWS = 8
WIDTH = 256


def with_ends(entries, stream_key, least, high):
    shape = entries.shape
    spot = [jax.random.randint(jax.random.fold_in(stream_key, axis), (), 0, shape[axis]) for axis in range(len(shape))]
    entries = entries.at[tuple(spot)].set(least)
    longest = shape.index(max(shape))
    spot[longest] = (spot[longest] + 1) % shape[longest]
    return entries.at[tuple(spot)].set(high)


def block_levels(stream_key, extent, split, least, high):
    level, own = 1.0, jax.random.fold_in(stream_key, 6)
    for dim, blocks in split:
        steps = jnp.exp(jax.random.uniform(jax.random.fold_in(own, dim), (blocks,), jnp.float32, least / len(split), high / len(split)))
        level = level * jnp.repeat(steps, extent[dim] // blocks).reshape([-1 if axis == dim else 1 for axis in range(len(extent))])
    return level


def noise(stream_key, dims, spread, limit, shards=(), held_as=jnp.bfloat16):
    array = jax.random.normal(stream_key, dims, jnp.float32) * spread
    if len(shards) > 0:
        array = block_levels(stream_key, dims, shards, -0.22, 0.18) * array
    return jnp.clip(array, min=-limit, max=limit).astype(held_as)


def setup_inputs(seed: int = 0, part: int = 0) -> dict:
    streams_of = jax.random.split(jax.random.key(seed), 9)
    part_splits = jax.random.split(jax.random.fold_in(streams_of[8], part), 9)
    latent = noise(part_splits[0], (HEIGHT, WIDTH, C), 1.0, 6.0, ((0, 2), (1, 8)), jnp.float32)
    offset = jax.random.randint(part_splits[1], (1,), 0, STRIDE).astype(jnp.int32)
    counts = with_ends(jax.random.randint(part_splits[2], (WINDOWS, 2 * STRIDE), 1, 5), jax.random.fold_in(part_splits[2], 1), 1, 4).astype(jnp.int32)
    conv_one = noise(streams_of[3], (3, 3, C, C), (9 * C) ** -0.5, 0.078125, ((3, 2),))
    conv_two = noise(streams_of[4], (3, 3, C, C), (9 * C) ** -0.5, 0.078125, ((3, 2),))
    gain_one = jnp.clip(1.0 + 0.18 * jax.random.normal(streams_of[5], (C,), jnp.float32), 0.1, 1.9)
    gain_two = jnp.clip(1.0 + 0.18 * jax.random.normal(streams_of[6], (C,), jnp.float32), 0.1, 1.9)
    time_bias = noise(streams_of[7], (C,), 1.0, 6.0, (), jnp.float32)
    return {"latent": latent, "offset": offset, "counts": counts, "conv_one": conv_one, "conv_two": conv_two, "gain_one": gain_one, "gain_two": gain_two, "time_bias": time_bias}


def nine_taps(framed, weight, height, columns):
    total = jnp.zeros((height * columns, weight.shape[3]), jnp.float32)
    for row_tap in range(3):
        for col_tap in range(3):
            patch = framed[row_tap:row_tap + height, col_tap:col_tap + columns]
            patch = patch.reshape(height * columns, framed.shape[2])
            total = total + jnp.dot(patch, weight[row_tap, col_tap], preferred_element_type=jnp.float32)
    return total

def group_silu(values, gain, size):
    grouped = values.reshape(values.shape[0], values.shape[1], values.shape[2] // size, size)
    count = values.shape[0] * values.shape[1] * size
    mean = lax.optimization_barrier(jnp.sum(grouped, axis=(0, 1, 3))) / count
    square = lax.optimization_barrier(jnp.sum(grouped * grouped, axis=(0, 1, 3))) / count
    scale = lax.rsqrt(square - mean * mean + 1e-05)
    normed = ((grouped - mean[:, None]) * scale[:, None]).reshape(values.shape) * gain
    return jax.nn.silu(normed).astype(jnp.bfloat16)

def reference(latent, offset, counts, conv_one, conv_two, gain_one, gain_two, time_bias):
    anchor = offset[0]
    width = latent.shape[1]
    channels = latent.shape[2]
    height = latent.shape[0]
    size = channels // GROUPS
    lowered = latent.astype(jnp.bfloat16)
    doubled = jnp.concatenate([lowered, lowered], axis=1)
    rolled = lax.dynamic_slice_in_dim(doubled, anchor, width, 1)
    blocks = rolled.reshape(height, WINDOWS, STRIDE, channels)
    windows = jnp.concatenate([blocks, jnp.roll(blocks, -1, axis=1)], axis=2)
    windows = jnp.transpose(windows, (1, 0, 2, 3))

    def denoise(window):
        source = window.astype(jnp.float32)
        columns = window.shape[1]
        act_one = group_silu(source, gain_one, size)
        framed = jnp.pad(act_one, ((1, 1), (1, 1), (0, 0)))
        hidden = nine_taps(framed, conv_one, height, columns).reshape(height, columns, channels) + time_bias
        act_two = group_silu(hidden, gain_two, size)
        framed = jnp.pad(act_two, ((1, 1), (1, 1), (0, 0)))
        return source + nine_taps(framed, conv_two, height, columns).reshape(height, columns, channels)
    prediction = lax.map(denoise, windows)
    weight = counts.astype(jnp.float32)
    numer = prediction * weight[:, None, :, None]
    numer_sum = numer[:, :, :STRIDE] + jnp.roll(numer[:, :, STRIDE:], 1, axis=0)
    weight_sum = weight[:, :STRIDE] + jnp.roll(weight[:, STRIDE:], 1, axis=0)
    joined_rolled = numer_sum / weight_sum[:, None, :, None]
    joined_rolled = jnp.transpose(joined_rolled, (1, 0, 2, 3)).reshape(height, width, channels)
    doubled_joined = jnp.concatenate([joined_rolled, joined_rolled], axis=1)
    joined = lax.dynamic_slice_in_dim(doubled_joined, width - anchor, width, 1)
    return math.sqrt(0.7 / 0.5) * (latent - math.sqrt(0.5) * joined) + math.sqrt(0.3) * joined
```

```python
import functools
import math

import jax
import jax.numpy as jnp
from jax import lax
from jax.experimental import pallas as pl
from jax.experimental.pallas import tpu as pltpu
from jax.sharding import PartitionSpec as P

GROUPS = 32
PARAMS = pltpu.CompilerParams(vmem_limit_bytes=20 * 2**20)
VMEM = pl.BlockSpec(memory_space=pltpu.VMEM)
SMEM = pl.BlockSpec(memory_space=pltpu.SMEM)
F32 = jnp.float32
BF16 = jnp.bfloat16


def moved(value, step, flip):
    blocks, cores = lax.axis_size("blk"), lax.axis_size("rows")
    pairs = [
        (b * cores + r, (step(b) % blocks) * cores + (r ^ flip))
        for b in range(blocks)
        for r in range(cores)
    ]
    return lax.ppermute(value, ("blk", "rows"), pairs)


def split3(x):
    high = x.astype(BF16)
    rest = x - high.astype(F32)
    mid = rest.astype(BF16)
    low = (rest - mid.astype(F32)).astype(BF16)
    return [high.astype(F32), mid.astype(F32), low.astype(F32)]


def regroup(first, second, table):
    rows = jnp.concatenate(split3(first) + split3(second) + [jnp.zeros_like(first)] * 2, axis=0)
    out = jnp.dot(rows.astype(BF16), table, preferred_element_type=F32)
    return out[0:1] + out[1:2] + out[2:3], out[3:4] + out[4:5] + out[5:6]


def group_scale(summed, squares, count, size):
    channels, lanes = summed.shape[1], 128
    ch = lax.broadcasted_iota(jnp.int32, (channels, lanes), 0)
    low = lax.broadcasted_iota(jnp.int32, (channels, lanes), 1) * size
    gather = jnp.where((ch >= low) & (ch < low + size), 1.0, 0.0).astype(BF16)
    ch = lax.broadcasted_iota(jnp.int32, (lanes, channels), 1)
    low = lax.broadcasted_iota(jnp.int32, (lanes, channels), 0) * size
    spread = jnp.where((ch >= low) & (ch < low + size), 1.0, 0.0).astype(BF16)
    total, total_sq = regroup(summed, squares, gather)
    mean = total / count
    scale = lax.rsqrt(total_sq / count - mean * mean + 1e-05)
    return regroup(mean, scale, spread)


def silu(u):
    half = 0.5 * u
    return half + half * jnp.tanh(half)


def nine_taps(frame, weight, acc):
    height, columns = frame.shape[0] - 2, frame.shape[1]
    for a in range(3):
        patch = frame[a : a + height].reshape(height * columns, frame.shape[2])
        taps = weight[a].reshape(-1, weight.shape[3])
        part = lax.dot_general(patch, taps, (((1,), (1,)), ((), ())), preferred_element_type=F32)
        if a == 0:
            acc[...] = part
        else:
            acc[...] += part


def joined_taps(acc, row, columns, outs, anchor):
    block = acc[row * columns : (row + 1) * columns]
    col = lax.broadcasted_iota(jnp.int32, (columns, outs), 0)
    left = pltpu.roll(block[:, :outs], 1, 0)
    right = pltpu.roll(block[:, 2 * outs :], columns - 1, 0)
    left = jnp.where(col == anchor, 0.0, left)
    right = jnp.where(col == ((anchor + columns - 1) & (columns - 1)), 0.0, right)
    return block[:, outs : 2 * outs] + left + right


def half_of(ref, outs, core):
    whole = ref[...].reshape(1, -1)
    return jnp.where(core == 0, whole[:, :outs], whole[:, outs:])


def first_kernel(size, anchor_ref, mix, mix_other, full, full_other, w, gain_one, time_bias, gain_two, out, frame, acc, hidden):
    core = lax.axis_index("rows")
    anchor = anchor_ref[0]
    rows, half_cols, channels = mix.shape
    columns, height, outs = 2 * half_cols, 2 * rows, out.shape[2]
    count = height * columns * size
    summed = jnp.zeros((1, channels), F32)
    squares = jnp.zeros((1, channels), F32)
    for ref in (mix, mix_other, full, full_other):
        v = ref[...].astype(F32).reshape(rows * half_cols, channels)
        summed += jnp.sum(v, axis=0, keepdims=True)
        squares += jnp.sum(v * v, axis=0, keepdims=True)
    mean, scale = group_scale(summed, squares, count, size)
    scale = scale * gain_one[...].reshape(1, -1)
    frame[0] = jnp.zeros(frame.shape[1:], BF16)
    frame[height + 1] = jnp.zeros(frame.shape[1:], BF16)
    for ref, mine, col in ((mix, 0, 0), (full, 0, half_cols), (mix_other, 1, 0), (full_other, 1, half_cols)):
        start = 1 + rows * (core ^ mine)
        for row in range(rows):
            v = ref[row].astype(F32)
            frame[start + row, col : col + half_cols] = silu((v - mean) * scale).astype(BF16)
    nine_taps(frame, w, acc)
    bias = half_of(time_bias, outs, core)
    summed = jnp.zeros((1, outs), F32)
    squares = jnp.zeros((1, outs), F32)
    for row in range(height):
        v = joined_taps(acc, row, columns, outs, anchor) + bias
        hidden[row] = v
        summed += jnp.sum(v, axis=0, keepdims=True)
        squares += jnp.sum(v * v, axis=0, keepdims=True)
    mean, scale = group_scale(summed, squares, count, size)
    scale = scale * half_of(gain_two, outs, core)
    for row in range(height):
        out[row] = silu((hidden[row] - mean) * scale).astype(BF16)


def second_kernel(anchor_ref, own, other, w, share, mix_same, mix_cross, full_same, full_cross, frame, acc, result):
    core = lax.axis_index("rows")
    anchor = anchor_ref[0]
    height, columns, outs = own.shape
    rows, half_cols = height // 2, columns // 2
    frame[0] = jnp.zeros(frame.shape[1:], BF16)
    frame[height + 1] = jnp.zeros(frame.shape[1:], BF16)

    @pl.when(core == 0)
    def _():
        for row in range(height):
            frame[1 + row] = jnp.concatenate([own[row], other[row]], axis=1)

    @pl.when(core == 1)
    def _():
        for row in range(height):
            frame[1 + row] = jnp.concatenate([other[row], own[row]], axis=1)

    nine_taps(frame, w, acc)
    part = jnp.broadcast_to(share[:, :1], (columns, outs))
    for row in range(height):
        result[row] = joined_taps(acc, row, columns, outs, anchor) * part
    for out, flip, col in (
        (mix_same, 0, 0),
        (mix_cross, 1, 0),
        (full_same, 0, half_cols),
        (full_cross, 1, half_cols),
    ):
        start = rows * (core ^ flip)
        for row in range(rows):
            out[row] = result[start + row, col : col + half_cols].astype(BF16)


def last_kernel(anchor_ref, latent, lowered, mix_own, mix_core, mix_same, mix_cross, full_same, full_cross, out):
    core = lax.axis_index("rows")
    odd = lax.axis_index("blk") & 1
    anchor = anchor_ref[0]
    rows, cols, outs = mix_own.shape
    col = lax.broadcasted_iota(jnp.int32, (cols, outs), 0)
    keep = (col >= anchor) ^ (odd == 1)
    own_scale = math.sqrt(0.7 / 0.5)
    join_scale = math.sqrt(0.3) - math.sqrt(0.7 / 0.5) * math.sqrt(0.5)
    for row in range(rows):
        same = jnp.where(keep, mix_own[row].astype(F32), mix_same[row].astype(F32)) + full_same[row].astype(F32)
        cross = jnp.where(keep, mix_core[row].astype(F32), mix_cross[row].astype(F32)) + full_cross[row].astype(F32)
        base = own_scale * latent[row] + join_scale * lowered[row].astype(F32)

        @pl.when(core == 0)
        def _():
            out[row] = base + join_scale * jnp.concatenate([same, cross], axis=1)

        @pl.when(core == 1)
        def _():
            out[row] = base + join_scale * jnp.concatenate([cross, same], axis=1)


def per_device(latent, offset, counts, conv_one, conv_two, gain_one, gain_two, time_bias):
    rows, stride, channels = latent.shape
    outs = conv_one.shape[3]
    size = channels // GROUPS
    height, columns = 2 * rows, 2 * stride
    odd = (lax.axis_index("blk") & 1) == 1
    first = lax.axis_index("rows") * outs
    anchor = offset[0]

    def computes(w):
        return w + 2 * (w % 2)

    lowered = latent.astype(BF16)
    full = moved(lowered, lambda b: b ^ 1, 0)
    beyond = moved(lowered, lambda b: b + 2 if b % 2 else b - 2, 0)
    row = counts[0].astype(F32)
    mine = moved(row, computes, 0)
    behind = moved(row, lambda w: computes(w + 1), 0)
    ahead = moved(row, lambda w: computes(w - 1), 0)
    share = mine / (mine + jnp.concatenate([behind[stride:], ahead[:stride]]))
    spot = lax.broadcasted_iota(jnp.int32, (columns, columns), 0) - anchor
    spot = jnp.where(spot < 0, spot + columns, spot)
    picked = spot == lax.broadcasted_iota(jnp.int32, (columns, columns), 1)
    share = jnp.sum(jnp.where(picked, share[None, :], 0.0), axis=1)
    share = jnp.broadcast_to(share[:, None], (columns, 128))
    full_other = moved(full, lambda b: b, 1)
    col = lax.broadcasted_iota(jnp.int32, lowered.shape, 1)
    mix = jnp.where((col >= anchor) ^ odd, lowered, beyond)
    mix_other = moved(mix, lambda b: b, 1)

    w_one = jnp.swapaxes(conv_one, 2, 3)
    w_two = jnp.swapaxes(conv_two, 2, 3)
    frame = pltpu.VMEM((height + 2, columns, channels), BF16)
    acc = pltpu.VMEM((height * columns, 3 * outs), F32)
    result = pltpu.VMEM((height, columns, outs), F32)
    own = pl.pallas_call(
        functools.partial(first_kernel, size),
        out_shape=jax.ShapeDtypeStruct((height, columns, outs), BF16),
        in_specs=[SMEM] + [VMEM] * 8,
        out_specs=VMEM,
        scratch_shapes=[frame, acc, result],
        compiler_params=PARAMS,
    )(offset, mix, mix_other, full, full_other, w_one, gain_one, time_bias, gain_two)
    other = moved(own, lambda b: b, 1)
    piece = jax.ShapeDtypeStruct((rows, stride, outs), BF16)
    mix_same, mix_cross, full_same, full_cross = pl.pallas_call(
        second_kernel,
        out_shape=(piece,) * 4,
        in_specs=[SMEM] + [VMEM] * 4,
        out_specs=(VMEM,) * 4,
        scratch_shapes=[frame, acc, result],
        compiler_params=PARAMS,
    )(offset, own, other, w_two, share)

    def aside(b):
        return b - 2 if b % 2 else b + 2

    got_full_same = moved(full_same, lambda b: b ^ 1, 0)
    got_full_cross = moved(full_cross, lambda b: b ^ 1, 1)
    got_mix_same = moved(mix_same, aside, 0)
    got_mix_cross = moved(mix_cross, aside, 1)
    got_core = moved(mix_cross, lambda b: b, 1)
    return pl.pallas_call(
        last_kernel,
        out_shape=jax.ShapeDtypeStruct(latent.shape, F32),
        in_specs=[SMEM] + [VMEM] * 8,
        out_specs=VMEM,
        compiler_params=PARAMS,
    )(offset, latent, lowered, mix_same, got_core, got_mix_same, got_mix_cross, got_full_same, got_full_cross)


def solution(mesh):
    return jax.shard_map(
        per_device,
        mesh=mesh,
        in_specs=(
            P(("pano", "rows"), "blk", None),
            P("pano"),
            P(("pano", "blk"), None),
            P(None, None, None, "rows"),
            P(None, None, None, "rows"),
            P(),
            P(),
            P(),
        ),
        out_specs=P(("pano", "rows"), "blk", None),
        check_vma=False,
    )
```

```python
import functools
import math

import jax
import jax.numpy as jnp
from jax import lax
from jax.experimental import pallas as pl
from jax.experimental.pallas import tpu as pltpu
from jax.sharding import PartitionSpec as P

GROUPS = 32
PARAMS = pltpu.CompilerParams(vmem_limit_bytes=20 * 2**20)
VMEM = pl.BlockSpec(memory_space=pltpu.VMEM)
HBM = pl.BlockSpec(memory_space=pltpu.HBM)
SMEM = pl.BlockSpec(memory_space=pltpu.SMEM)
F32 = jnp.float32
BF16 = jnp.bfloat16


def moved(value, step, flip):
    blocks, cores = lax.axis_size("blk"), lax.axis_size("rows")
    pairs = [
        (b * cores + r, (step(b) % blocks) * cores + (r ^ flip))
        for b in range(blocks)
        for r in range(cores)
    ]
    return lax.ppermute(value, ("blk", "rows"), pairs)


def split3(x):
    high = x.astype(BF16)
    rest = x - high.astype(F32)
    mid = rest.astype(BF16)
    low = (rest - mid.astype(F32)).astype(BF16)
    return [high.astype(F32), mid.astype(F32), low.astype(F32)]


def regroup(first, second, table):
    rows = jnp.concatenate(split3(first) + split3(second) + [jnp.zeros_like(first)] * 2, axis=0)
    out = jnp.dot(rows.astype(BF16), table, preferred_element_type=F32)
    return out[0:1] + out[1:2] + out[2:3], out[3:4] + out[4:5] + out[5:6]


def group_scale(summed, squares, count, size):
    channels, lanes = summed.shape[1], 128
    ch = lax.broadcasted_iota(jnp.int32, (channels, lanes), 0)
    low = lax.broadcasted_iota(jnp.int32, (channels, lanes), 1) * size
    gather = jnp.where((ch >= low) & (ch < low + size), 1.0, 0.0).astype(BF16)
    ch = lax.broadcasted_iota(jnp.int32, (lanes, channels), 1)
    low = lax.broadcasted_iota(jnp.int32, (lanes, channels), 0) * size
    spread = jnp.where((ch >= low) & (ch < low + size), 1.0, 0.0).astype(BF16)
    total, total_sq = regroup(summed, squares, gather)
    mean = total / count
    scale = lax.rsqrt(total_sq / count - mean * mean + 1e-05)
    return regroup(mean, scale, spread)


def silu(u):
    half = 0.5 * u
    return half + half * jnp.tanh(half)


def nine_taps(frame, weight, acc, arriving=()):
    height, columns = frame.shape[0] - 2, frame.shape[1]
    for a in range(3):
        if arriving:
            arriving[a].wait()
        patch = frame[a : a + height].reshape(height * columns, frame.shape[2])
        taps = weight[a].reshape(-1, weight.shape[3])
        part = lax.dot_general(patch, taps, (((1,), (1,)), ((), ())), preferred_element_type=F32)
        if a == 0:
            acc[...] = part
        else:
            acc[...] += part


def joined_taps(acc, row, columns, outs, edges):
    block = acc[row * columns : (row + 1) * columns]
    left = pltpu.roll(block[:, :outs], 1, 0) * edges[0][:, :1]
    right = pltpu.roll(block[:, 2 * outs :], columns - 1, 0) * edges[1][:, :1]
    return block[:, outs : 2 * outs] + left + right


def half_of(row, outs, core):
    return jnp.where(core == 0, row[:, :outs], row[:, outs:])


def first_kernel(size, mix, mix_other, full, full_other, edges, w_one, w_two, gain_one, gain_two, time_bias, out, w_next, frame, acc, hidden, w, one_in, two_in, bias_in, sems):
    core = lax.axis_index("rows")
    small = [
        pltpu.make_async_copy(source, target, sems.at[4 + i])
        for i, (source, target) in enumerate(((gain_one, one_in), (gain_two, two_in), (time_bias, bias_in)))
    ]
    taps = [pltpu.make_async_copy(w_one.at[a], w.at[a], sems.at[a]) for a in range(3)]
    later = pltpu.make_async_copy(w_two, w_next, sems.at[3])
    for copy in small + taps + [later]:
        copy.start()
    rows, half_cols, channels = mix.shape
    columns, height, outs = 2 * half_cols, 2 * rows, out.shape[2]
    count = height * columns * size
    summed = jnp.zeros((1, channels), F32)
    squares = jnp.zeros((1, channels), F32)
    for ref in (mix, mix_other, full, full_other):
        v = ref[...].astype(F32).reshape(rows * half_cols, channels)
        summed += jnp.sum(v, axis=0, keepdims=True)
        squares += jnp.sum(v * v, axis=0, keepdims=True)
    mean, scale = group_scale(summed, squares, count, size)
    for copy in small:
        copy.wait()
    scale = scale * one_in[...].reshape(1, -1)
    frame[0] = jnp.zeros(frame.shape[1:], BF16)
    frame[height + 1] = jnp.zeros(frame.shape[1:], BF16)
    for ref, mine, col in ((mix, 0, 0), (full, 0, half_cols), (mix_other, 1, 0), (full_other, 1, half_cols)):
        start = 1 + rows * (core ^ mine)
        for row in range(rows):
            v = ref[row].astype(F32)
            frame[start + row, col : col + half_cols] = silu((v - mean) * scale).astype(BF16)
    nine_taps(frame, w, acc, taps)
    bias = half_of(bias_in[...].reshape(1, -1), outs, core)
    summed = jnp.zeros((1, outs), F32)
    squares = jnp.zeros((1, outs), F32)
    for row in range(height):
        v = joined_taps(acc, row, columns, outs, edges) + bias
        hidden[row] = v
        summed += jnp.sum(v, axis=0, keepdims=True)
        squares += jnp.sum(v * v, axis=0, keepdims=True)
    mean, scale = group_scale(summed, squares, count, size)
    scale = scale * half_of(two_in[...].reshape(1, -1), outs, core)
    for row in range(height):
        out[row] = silu((hidden[row] - mean) * scale).astype(BF16)
    later.wait()


def second_kernel(own, other, w, edges, share, mix_same, mix_cross, full_same, full_cross, frame, acc, result):
    core = lax.axis_index("rows")
    height, columns, outs = own.shape
    rows, half_cols = height // 2, columns // 2
    frame[0] = jnp.zeros(frame.shape[1:], BF16)
    frame[height + 1] = jnp.zeros(frame.shape[1:], BF16)

    @pl.when(core == 0)
    def _():
        for row in range(height):
            frame[1 + row] = jnp.concatenate([own[row], other[row]], axis=1)

    @pl.when(core == 1)
    def _():
        for row in range(height):
            frame[1 + row] = jnp.concatenate([other[row], own[row]], axis=1)

    nine_taps(frame, w, acc)
    part = jnp.broadcast_to(share[:, :1], (columns, outs))
    for row in range(height):
        result[row] = joined_taps(acc, row, columns, outs, edges) * part
    for out, flip, col in (
        (mix_same, 0, 0),
        (mix_cross, 1, 0),
        (full_same, 0, half_cols),
        (full_cross, 1, half_cols),
    ):
        start = rows * (core ^ flip)
        for row in range(rows):
            out[row] = result[start + row, col : col + half_cols].astype(BF16)


def last_kernel(latent, lowered, edges, inverse, mix_own, mix_core, mix_same, mix_cross, full_same, full_cross, out):
    core = lax.axis_index("rows")
    odd = lax.axis_index("blk") & 1
    rows, cols, outs = mix_own.shape
    late = jnp.broadcast_to(edges[2, :cols, :1], (cols, outs)) > 0.5
    keep = late ^ (odd == 1)
    own_scale = math.sqrt(0.7 / 0.5)
    join_scale = math.sqrt(0.3) - math.sqrt(0.7 / 0.5) * math.sqrt(0.5)
    part = join_scale * inverse[:, :1]
    for row in range(rows):
        same = jnp.where(keep, mix_own[row].astype(F32), mix_same[row].astype(F32)) + full_same[row].astype(F32)
        cross = jnp.where(keep, mix_core[row].astype(F32), mix_cross[row].astype(F32)) + full_cross[row].astype(F32)
        base = own_scale * latent[row] + join_scale * lowered[row].astype(F32)

        @pl.when(core == 0)
        def _():
            out[row] = base + part * jnp.concatenate([same, cross], axis=1)

        @pl.when(core == 1)
        def _():
            out[row] = base + part * jnp.concatenate([cross, same], axis=1)


def by_column(values, anchor):
    columns = values.shape[0]
    spot = lax.broadcasted_iota(jnp.int32, (columns, columns), 0) - anchor
    spot = jnp.where(spot < 0, spot + columns, spot)
    picked = spot == lax.broadcasted_iota(jnp.int32, (columns, columns), 1)
    placed = jnp.sum(jnp.where(picked, values[None, :], 0.0), axis=1)
    return jnp.broadcast_to(placed[:, None], (columns, 128))


def per_device(latent, offset, counts, conv_one, conv_two, gain_one, gain_two, time_bias):
    rows, stride, channels = latent.shape
    outs = conv_one.shape[3]
    size = channels // GROUPS
    height, columns = 2 * rows, 2 * stride
    odd = (lax.axis_index("blk") & 1) == 1
    anchor = offset[0]

    lowered = lax.optimization_barrier(latent.astype(BF16))
    full = moved(lowered, lambda b: b ^ 1, 0)
    beyond = moved(lowered, lambda b: b + 2 if b % 2 else b - 2, 0)
    row = counts[0].astype(F32)
    row_one = moved(row, lambda b: b + 1, 0)
    row_two = moved(row, lambda b: b + 2, 0)
    share = by_column(jnp.where(odd, row_two, row), anchor)
    now = by_column(row, anchor)[:stride]
    then = by_column(row_two, anchor)[:stride]
    always = by_column(row_one, anchor)[stride:]
    col = lax.broadcasted_iota(jnp.int32, (stride, 1), 0)
    inverse = 1.0 / (always + jnp.where(col >= anchor, now, then))

    spot = lax.broadcasted_iota(jnp.int32, (3, columns, 128), 1)
    kind = lax.broadcasted_iota(jnp.int32, (3, columns, 128), 0)
    cut = jnp.where(kind == 0, spot == anchor, spot == jnp.where(anchor == 0, columns, anchor) - 1)
    edges = jnp.where(jnp.where(kind == 2, spot < anchor, cut), 0.0, 1.0)

    full_other = moved(full, lambda b: b, 1)
    col = lax.broadcasted_iota(jnp.int32, lowered.shape, 1)
    mix = jnp.where((col >= anchor) ^ odd, lowered, beyond)
    mix_other = moved(mix, lambda b: b, 1)

    frame = pltpu.VMEM((height + 2, columns, channels), BF16)
    acc = pltpu.VMEM((height * columns, 3 * outs), F32)
    result = pltpu.VMEM((height, columns, outs), F32)
    weights = (3, 3, outs, channels)
    own, w_next = pl.pallas_call(
        functools.partial(first_kernel, size),
        out_shape=(
            jax.ShapeDtypeStruct((height, columns, outs), BF16),
            jax.ShapeDtypeStruct(weights, BF16),
        ),
        in_specs=[VMEM] * 5 + [HBM] * 5,
        out_specs=(VMEM, VMEM),
        scratch_shapes=[
            frame,
            acc,
            result,
            pltpu.VMEM(weights, BF16),
            pltpu.VMEM((channels,), F32),
            pltpu.VMEM((channels,), F32),
            pltpu.VMEM((channels,), F32),
            pltpu.SemaphoreType.DMA((7,)),
        ],
        compiler_params=PARAMS,
    )(mix, mix_other, full, full_other, edges, *[
        pltpu.with_memory_space_constraint(v, pltpu.HBM)
        for v in (jnp.swapaxes(conv_one, 2, 3), jnp.swapaxes(conv_two, 2, 3), gain_one, gain_two, time_bias)
    ])
    other = moved(own, lambda b: b, 1)
    piece = jax.ShapeDtypeStruct((rows, stride, outs), BF16)
    mix_same, mix_cross, full_same, full_cross = pl.pallas_call(
        second_kernel,
        out_shape=(piece,) * 4,
        in_specs=[VMEM] * 5,
        out_specs=(VMEM,) * 4,
        scratch_shapes=[frame, acc, result],
        compiler_params=PARAMS,
    )(own, other, w_next, edges, share)

    def aside(b):
        return b - 2 if b % 2 else b + 2

    got_mix_same = moved(mix_same, aside, 0)
    got_mix_cross = moved(mix_cross, aside, 1)
    got_full_same = moved(full_same, lambda b: b ^ 1, 0)
    got_full_cross = moved(full_cross, lambda b: b ^ 1, 1)
    got_core = moved(mix_cross, lambda b: b, 1)
    return pl.pallas_call(
        last_kernel,
        out_shape=jax.ShapeDtypeStruct(latent.shape, F32),
        in_specs=[VMEM] * 10,
        out_specs=VMEM,
        compiler_params=PARAMS,
    )(latent, lowered, edges, inverse, mix_same, got_core, got_mix_same, got_mix_cross, got_full_same, got_full_cross)


def solution(mesh):
    return jax.shard_map(
        per_device,
        mesh=mesh,
        in_specs=(
            P(("pano", "rows"), "blk", None),
            P("pano"),
            P(("pano", "blk"), None),
            P(None, None, None, "rows"),
            P(None, None, None, "rows"),
            P(),
            P(),
            P(),
        ),
        out_specs=P(("pano", "rows"), "blk", None),
        check_vma=False,
    )
```

```python
import functools
import math

import jax
import jax.numpy as jnp
from jax import lax
from jax.experimental import pallas as pl
from jax.experimental.pallas import tpu as pltpu
from jax.sharding import PartitionSpec as P

GROUPS = 32
PARAMS = pltpu.CompilerParams(vmem_limit_bytes=20 * 2**20)
VMEM = pl.BlockSpec(memory_space=pltpu.VMEM)
HBM = pl.BlockSpec(memory_space=pltpu.HBM)
SMEM = pl.BlockSpec(memory_space=pltpu.SMEM)
F32 = jnp.float32
BF16 = jnp.bfloat16


def moved(value, step, flip):
    blocks, cores = lax.axis_size("blk"), lax.axis_size("rows")
    pairs = [
        (b * cores + r, (step(b) % blocks) * cores + (r ^ flip))
        for b in range(blocks)
        for r in range(cores)
    ]
    return lax.ppermute(value, ("blk", "rows"), pairs)


def split3(x):
    high = x.astype(BF16)
    rest = x - high.astype(F32)
    mid = rest.astype(BF16)
    low = (rest - mid.astype(F32)).astype(BF16)
    return [high.astype(F32), mid.astype(F32), low.astype(F32)]


def regroup(first, second, table):
    rows = jnp.concatenate(split3(first) + split3(second) + [jnp.zeros_like(first)] * 2, axis=0)
    out = jnp.dot(rows.astype(BF16), table, preferred_element_type=F32)
    return out[0:1] + out[1:2] + out[2:3], out[3:4] + out[4:5] + out[5:6]


def group_scale(summed, squares, count, size):
    channels, lanes = summed.shape[1], 128
    ch = lax.broadcasted_iota(jnp.int32, (channels, lanes), 0)
    low = lax.broadcasted_iota(jnp.int32, (channels, lanes), 1) * size
    gather = jnp.where((ch >= low) & (ch < low + size), 1.0, 0.0).astype(BF16)
    ch = lax.broadcasted_iota(jnp.int32, (lanes, channels), 1)
    low = lax.broadcasted_iota(jnp.int32, (lanes, channels), 0) * size
    spread = jnp.where((ch >= low) & (ch < low + size), 1.0, 0.0).astype(BF16)
    total, total_sq = regroup(summed, squares, gather)
    mean = total / count
    scale = lax.rsqrt(total_sq / count - mean * mean + 1e-05)
    return regroup(mean, scale, spread)


def silu(u):
    half = 0.5 * u
    return half + half * jnp.tanh(half)


def nine_taps(frame, weight, acc):
    height, columns = frame.shape[0] - 2, frame.shape[1]
    for a in range(3):
        patch = frame[a : a + height].reshape(height * columns, frame.shape[2])
        taps = weight[a].reshape(-1, weight.shape[3])
        part = lax.dot_general(patch, taps, (((1,), (1,)), ((), ())), preferred_element_type=F32)
        if a == 0:
            acc[...] = part
        else:
            acc[...] += part


def joined_taps(acc, row, columns, outs, edges):
    block = acc[row * columns : (row + 1) * columns]
    left = pltpu.roll(block[:, :outs], 1, 0) * edges[0][:, :1]
    right = pltpu.roll(block[:, 2 * outs :], columns - 1, 0) * edges[1][:, :1]
    return block[:, outs : 2 * outs] + left + right


TAIL = 8


def packed(rows, columns, outs, tail=0):
    return jax.ShapeDtypeStruct((rows * columns // 2 + tail, 2 * outs), BF16)


def put(ref, row, rows, value):
    half, outs, columns = rows // 2, ref.shape[1] // 2, value.shape[0]
    spot = (row % half) * columns
    ref[spot : spot + columns, (row // half) * outs : (row // half + 1) * outs] = value


def get(ref, row, rows, columns):
    half, outs = rows // 2, ref.shape[1] // 2
    spot = (row % half) * columns
    return ref[spot : spot + columns, (row // half) * outs : (row // half + 1) * outs]


def half_of(row, outs, core):
    return jnp.where(core == 0, row[:, :outs], row[:, outs:])


def lower_kernel(latent, counts, lowered, load, held, counted, sems):
    rows, cols, _ = latent.shape
    copies = [pltpu.make_async_copy(latent.at[row], held.at[row], sems.at[row]) for row in range(rows)]
    copies.append(pltpu.make_async_copy(counts, counted, sems.at[rows]))
    for copy in copies:
        copy.start()
    for row in range(rows):
        copies[row].wait()
        value = held[row].astype(BF16)
        lowered[row] = value
        load[row * cols : (row + 1) * cols] = value
    copies[rows].wait()
    put_counts(load, rows * cols, counted[...].astype(F32))


def ready_kernel(w_one, w, sem):
    copy = pltpu.make_async_copy(w_one, w, sem)
    copy.start()
    copy.wait()


def put_counts(ref, start, row):
    tail = ref.shape[0] - start
    room = ref.shape[1] - row.shape[1]
    wide = jnp.concatenate([row, jnp.zeros((1, room), F32)], axis=1)
    ref[start:] = jnp.broadcast_to(wide, (tail, ref.shape[1])).astype(BF16)


def get_counts(ref, start, columns):
    return ref[start : start + 8].astype(F32)[:1, :columns]


def by_column(values, anchor, columns):
    spot = lax.broadcasted_iota(jnp.int32, (columns, columns), 0) - anchor
    spot = jnp.where(spot < 0, spot + columns, spot)
    picked = spot == lax.broadcasted_iota(jnp.int32, (columns, columns), 1)
    return jnp.sum(jnp.where(picked, values, 0.0), axis=1, keepdims=True)


def first_kernel(size, mix, mix_other, full, full_other, edges, w, w_two, gain_one, gain_two, time_bias, out, w_next, frame, acc, hidden, one_in, two_in, bias_in, sems):
    core = lax.axis_index("rows")
    small = [
        pltpu.make_async_copy(source, target, sems.at[1 + i])
        for i, (source, target) in enumerate(((gain_one, one_in), (gain_two, two_in), (time_bias, bias_in)))
    ]
    later = pltpu.make_async_copy(w_two, w_next, sems.at[0])
    for copy in small + [later]:
        copy.start()
    rows, half_cols, channels = mix.shape
    columns, height, outs = 2 * half_cols, 2 * rows, out.shape[1] // 2
    count = height * columns * size
    summed = jnp.zeros((1, channels), F32)
    squares = jnp.zeros((1, channels), F32)
    for ref in (mix, mix_other, full, full_other):
        v = ref[...].astype(F32).reshape(rows * half_cols, channels)
        summed += jnp.sum(v, axis=0, keepdims=True)
        squares += jnp.sum(v * v, axis=0, keepdims=True)
    mean, scale = group_scale(summed, squares, count, size)
    for copy in small:
        copy.wait()
    scale = scale * one_in[...].reshape(1, -1)
    frame[0] = jnp.zeros(frame.shape[1:], BF16)
    frame[height + 1] = jnp.zeros(frame.shape[1:], BF16)
    for ref, mine, col in ((mix, 0, 0), (full, 0, half_cols), (mix_other, 1, 0), (full_other, 1, half_cols)):
        start = 1 + rows * (core ^ mine)
        for row in range(rows):
            v = ref[row].astype(F32)
            frame[start + row, col : col + half_cols] = silu((v - mean) * scale).astype(BF16)
    nine_taps(frame, w, acc)
    bias = half_of(bias_in[...].reshape(1, -1), outs, core)
    summed = jnp.zeros((1, outs), F32)
    squares = jnp.zeros((1, outs), F32)
    for row in range(height):
        v = joined_taps(acc, row, columns, outs, edges) + bias
        hidden[row] = v
        summed += jnp.sum(v, axis=0, keepdims=True)
        squares += jnp.sum(v * v, axis=0, keepdims=True)
    mean, scale = group_scale(summed, squares, count, size)
    scale = scale * half_of(two_in[...].reshape(1, -1), outs, core)
    for row in range(height):
        put(out, row, height, silu((hidden[row] - mean) * scale).astype(BF16))
    later.wait()


def second_kernel(anchor_ref, own, other, w, edges, counts, load, mix_same, mix_cross, full_same, full_cross, frame, acc, result):
    core = lax.axis_index("rows")
    odd = (lax.axis_index("blk") & 1) == 1
    height, columns = frame.shape[0] - 2, frame.shape[1]
    outs = own.shape[1] // 2
    rows, half_cols = height // 2, columns // 2
    frame[0] = jnp.zeros(frame.shape[1:], BF16)
    frame[height + 1] = jnp.zeros(frame.shape[1:], BF16)

    @pl.when(core == 0)
    def _():
        for row in range(height):
            frame[1 + row] = jnp.concatenate([get(ref, row, height, columns) for ref in (own, other)], axis=1)

    @pl.when(core == 1)
    def _():
        for row in range(height):
            frame[1 + row] = jnp.concatenate([get(ref, row, height, columns) for ref in (other, own)], axis=1)

    nine_taps(frame, w, acc)
    own_row = jnp.where(odd, get_counts(load, rows * half_cols, columns), counts[...].astype(F32))
    part = jnp.broadcast_to(by_column(own_row, anchor_ref[0], columns), (columns, outs))
    for row in range(height):
        result[row] = joined_taps(acc, row, columns, outs, edges) * part
    for out, flip, col in (
        (mix_same, 0, 0),
        (mix_cross, 1, 0),
        (full_same, 0, half_cols),
        (full_cross, 1, half_cols),
    ):
        start = rows * (core ^ flip)
        for row in range(rows):
            put(out, row, rows, result[start + row, col : col + half_cols].astype(BF16))
    for out in (mix_same, full_same):
        put_counts(out, rows * half_cols // 2, own_row)


def last_kernel(anchor_ref, latent, lowered, counts, load, mix_own, mix_core, mix_same, mix_cross, full_same, full_cross, out, done, sems):
    core = lax.axis_index("rows")
    odd = (lax.axis_index("blk") & 1) == 1
    anchor = anchor_ref[0]
    rows, cols, outs = latent.shape[0], latent.shape[1], latent.shape[2] // 2
    late = lax.broadcasted_iota(jnp.int32, (cols, outs), 0) >= anchor
    keep = late ^ odd
    tail = rows * cols // 2
    own_row = jnp.where(odd, get_counts(load, rows * cols, 2 * cols), counts[...].astype(F32))
    always = by_column(get_counts(full_same, tail, 2 * cols), anchor, 2 * cols)[cols:]
    ours = by_column(own_row, anchor, 2 * cols)[:cols]
    theirs = by_column(get_counts(mix_same, tail, 2 * cols), anchor, 2 * cols)[:cols]
    weight = always + jnp.where(keep[:, :1], ours, theirs)
    own_scale = math.sqrt(0.7 / 0.5)
    join_scale = math.sqrt(0.3) - math.sqrt(0.7 / 0.5) * math.sqrt(0.5)
    part = join_scale / weight

    copies = [pltpu.make_async_copy(done.at[row], out.at[row], sems.at[row]) for row in range(rows)]

    def summed(row, own, far, full):
        own, far, full = (get(ref, row, rows, cols).astype(F32) for ref in (own, far, full))
        return jnp.where(keep, own, far) + full

    for row in range(rows):
        same = summed(row, mix_own, mix_same, full_same)
        cross = summed(row, mix_core, mix_cross, full_cross)
        base = own_scale * latent[row] + join_scale * lowered[row].astype(F32)

        @pl.when(core == 0)
        def _():
            done[row] = base + part * jnp.concatenate([same, cross], axis=1)

        @pl.when(core == 1)
        def _():
            done[row] = base + part * jnp.concatenate([cross, same], axis=1)

        copies[row].start()
    for copy in copies:
        copy.wait()


def in_hbm(value):
    return pltpu.with_memory_space_constraint(value, pltpu.HBM)


def per_device(latent, offset, counts, conv_one, conv_two, gain_one, gain_two, time_bias):
    rows, stride, channels = latent.shape
    outs = conv_one.shape[3]
    size = channels // GROUPS
    height, columns = 2 * rows, 2 * stride
    odd = (lax.axis_index("blk") & 1) == 1
    anchor = offset[0]

    conv_one, conv_two = (jnp.swapaxes(v, 2, 3) for v in (conv_one, conv_two))
    lowered, load, held, counted = pl.pallas_call(
        lower_kernel,
        out_shape=(
            jax.ShapeDtypeStruct(latent.shape, BF16),
            jax.ShapeDtypeStruct((rows * stride + TAIL, channels), BF16),
            jax.ShapeDtypeStruct(latent.shape, F32),
            jax.ShapeDtypeStruct(counts.shape, counts.dtype),
        ),
        in_specs=[HBM] * 2,
        out_specs=(VMEM,) * 4,
        scratch_shapes=[pltpu.SemaphoreType.DMA((rows + 1,))],
        compiler_params=PARAMS,
    )(in_hbm(latent), in_hbm(counts))
    w_first = pl.pallas_call(
        ready_kernel,
        out_shape=jax.ShapeDtypeStruct(conv_one.shape, BF16),
        in_specs=[HBM],
        out_specs=VMEM,
        scratch_shapes=[pltpu.SemaphoreType.DMA],
        compiler_params=PARAMS,
    )(in_hbm(conv_one))
    full = moved(lowered, lambda b: b ^ 1, 0)
    load = moved(load, lambda b: b + 2 if b % 2 else b - 2, 0)
    beyond = load[: rows * stride].reshape(latent.shape)
    spot = lax.broadcasted_iota(jnp.int32, (3, columns, 128), 1)
    kind = lax.broadcasted_iota(jnp.int32, (3, columns, 128), 0)
    cut = jnp.where(kind == 0, spot == anchor, spot == jnp.where(anchor == 0, columns, anchor) - 1)
    edges = jnp.where(jnp.where(kind == 2, spot < anchor, cut), 0.0, 1.0)

    full_other = moved(full, lambda b: b, 1)
    col = lax.broadcasted_iota(jnp.int32, lowered.shape, 1)
    mix = jnp.where((col >= anchor) ^ odd, lowered, beyond)
    mix_other = moved(mix, lambda b: b, 1)

    frame = pltpu.VMEM((height + 2, columns, channels), BF16)
    acc = pltpu.VMEM((height * columns, 3 * outs), F32)
    result = pltpu.VMEM((height, columns, outs), F32)
    weights = (3, 3, outs, channels)
    own, w_next = pl.pallas_call(
        functools.partial(first_kernel, size),
        out_shape=(
            packed(height, columns, outs),
            jax.ShapeDtypeStruct(weights, BF16),
        ),
        in_specs=[VMEM] * 6 + [HBM] * 4,
        out_specs=(VMEM, VMEM),
        scratch_shapes=[
            frame,
            acc,
            result,
            pltpu.VMEM((channels,), F32),
            pltpu.VMEM((channels,), F32),
            pltpu.VMEM((channels,), F32),
            pltpu.SemaphoreType.DMA((4,)),
        ],
        compiler_params=PARAMS,
    )(mix, mix_other, full, full_other, edges, w_first, *[in_hbm(v) for v in (conv_two, gain_one, gain_two, time_bias)])
    other = moved(own, lambda b: b, 1)
    marked, plain = packed(rows, stride, outs, TAIL), packed(rows, stride, outs)
    mix_same, mix_cross, full_same, full_cross = pl.pallas_call(
        second_kernel,
        out_shape=(marked, plain, marked, plain),
        in_specs=[SMEM] + [VMEM] * 6,
        out_specs=(VMEM,) * 4,
        scratch_shapes=[frame, acc, result],
        compiler_params=PARAMS,
    )(offset, own, other, w_next, edges, counted, load)

    def aside(b):
        return b - 2 if b % 2 else b + 2

    got_mix_same = moved(mix_same, aside, 0)
    got_mix_cross = moved(mix_cross, aside, 1)
    got_full_same = moved(full_same, lambda b: b ^ 1, 0)
    got_full_cross = moved(full_cross, lambda b: b ^ 1, 1)
    got_core = moved(mix_cross, lambda b: b, 1)
    return pl.pallas_call(
        last_kernel,
        out_shape=jax.ShapeDtypeStruct(latent.shape, F32),
        in_specs=[SMEM] + [VMEM] * 10,
        out_specs=HBM,
        scratch_shapes=[pltpu.VMEM(latent.shape, F32), pltpu.SemaphoreType.DMA((rows,))],
        compiler_params=PARAMS,
    )(offset, held, lowered, counted, load, mix_same, got_core, got_mix_same, got_mix_cross, got_full_same, got_full_cross)


def solution(mesh):
    return jax.shard_map(
        per_device,
        mesh=mesh,
        in_specs=(
            P(("pano", "rows"), "blk", None),
            P("pano"),
            P(("pano", "blk"), None),
            P(None, None, None, "rows"),
            P(None, None, None, "rows"),
            P(),
            P(),
            P(),
        ),
        out_specs=P(("pano", "rows"), "blk", None),
        check_vma=False,
    )
```

```python
import functools
import math

import jax
import jax.numpy as jnp
from jax import lax
from jax.experimental import pallas as pl
from jax.experimental.pallas import tpu as pltpu
from jax.sharding import PartitionSpec as P

GROUPS = 32
PARAMS = pltpu.CompilerParams(vmem_limit_bytes=20 * 2**20)
VMEM = pl.BlockSpec(memory_space=pltpu.VMEM)
HBM = pl.BlockSpec(memory_space=pltpu.HBM)
SMEM = pl.BlockSpec(memory_space=pltpu.SMEM)
F32 = jnp.float32
BF16 = jnp.bfloat16


def moved(value, step, flip):
    blocks, cores = lax.axis_size("blk"), lax.axis_size("rows")
    pairs = [
        (b * cores + r, (step(b) % blocks) * cores + (r ^ flip))
        for b in range(blocks)
        for r in range(cores)
    ]
    return lax.ppermute(value, ("blk", "rows"), pairs)


def split3(x):
    high = x.astype(BF16)
    rest = x - high.astype(F32)
    mid = rest.astype(BF16)
    low = (rest - mid.astype(F32)).astype(BF16)
    return [high.astype(F32), mid.astype(F32), low.astype(F32)]


def regroup(first, second, table):
    rows = jnp.concatenate(split3(first) + split3(second) + [jnp.zeros_like(first)] * 2, axis=0)
    out = jnp.dot(rows.astype(BF16), table, preferred_element_type=F32)
    return out[0:1] + out[1:2] + out[2:3], out[3:4] + out[4:5] + out[5:6]


def group_scale(summed, squares, count, size):
    channels, lanes = summed.shape[1], 128
    ch = lax.broadcasted_iota(jnp.int32, (channels, lanes), 0)
    low = lax.broadcasted_iota(jnp.int32, (channels, lanes), 1) * size
    gather = jnp.where((ch >= low) & (ch < low + size), 1.0, 0.0).astype(BF16)
    ch = lax.broadcasted_iota(jnp.int32, (lanes, channels), 1)
    low = lax.broadcasted_iota(jnp.int32, (lanes, channels), 0) * size
    spread = jnp.where((ch >= low) & (ch < low + size), 1.0, 0.0).astype(BF16)
    total, total_sq = regroup(summed, squares, gather)
    mean = total / count
    scale = lax.rsqrt(total_sq / count - mean * mean + 1e-05)
    return regroup(mean, scale, spread)


def silu(u):
    half = 0.5 * u
    return half + half * jnp.tanh(half)


def arranged(weight, target, sem):
    outs = weight.shape[2]
    whole = outs // 128 * 128
    copies, start = [], 0
    for part in (slice(0, whole), slice(whole, outs)):
        for b in range(3):
            size = part.stop - part.start
            for a in range(3):
                spot = target.at[a, start : start + size]
                copies.append(pltpu.make_async_copy(weight.at[a, b, part], spot, sem.at[len(copies)]))
            start += size
    return copies


def nine_taps(frame, weight, acc, first=None):
    height, columns, channels = frame.shape[0] - 2, frame.shape[1], frame.shape[2]
    patch = jnp.concatenate(
        [frame[a : a + height].reshape(height * columns, channels) for a in range(3)], axis=1
    )
    some = slice(None) if first is None else pl.ds(pl.multiple_of(first, 128), channels)
    taps = jnp.concatenate([weight[a, :, some] for a in range(3)], axis=1)
    acc[...] = lax.dot_general(patch, taps, (((1,), (1,)), ((), ())), preferred_element_type=F32)


def joined_taps(acc, row, columns, outs, edges):
    block = acc[row * columns : (row + 1) * columns]
    whole = outs // 128 * 128

    def joined(start, width):
        first, second, third = (block[:, start + b * width : start + (b + 1) * width] for b in range(3))
        cuts = [jnp.concatenate([edges[b]] * pl.cdiv(width, 128), axis=1)[:, :width] for b in range(2)]
        return second + pltpu.roll(first, 1, 0) * cuts[0] + pltpu.roll(third, columns - 1, 0) * cuts[1]

    return jnp.concatenate([joined(0, whole), joined(3 * whole, outs - whole)], axis=1)


TAIL = 8


def packed(rows, columns, outs, tail=0):
    return jax.ShapeDtypeStruct((rows * columns // 2 + tail, 2 * outs), BF16)


def put(ref, row, rows, value):
    half, outs, columns = rows // 2, ref.shape[1] // 2, value.shape[0]
    spot = (row % half) * columns
    ref[spot : spot + columns, (row // half) * outs : (row // half + 1) * outs] = value


def get(ref, row, rows, columns):
    half, outs = rows // 2, ref.shape[1] // 2
    spot = (row % half) * columns
    return ref[spot : spot + columns, (row // half) * outs : (row // half + 1) * outs]


def half_of(row, outs, core):
    return jnp.where(core == 0, row[:, :outs], row[:, outs:])


def lower_kernel(latent, counts, lowered, load, held, counted, sems):
    rows, cols, _ = latent.shape
    copies = [pltpu.make_async_copy(latent.at[row], held.at[row], sems.at[row]) for row in range(rows)]
    copies.append(pltpu.make_async_copy(counts, counted, sems.at[rows]))
    for copy in copies:
        copy.start()
    for row in range(rows):
        copies[row].wait()
        value = held[row].astype(BF16)
        lowered[row] = value
        load[row * cols : (row + 1) * cols] = value
    copies[rows].wait()
    put_counts(load, rows * cols, counted[...].astype(F32))


def ready_kernel(w_one, w_two, gain_one, gain_two, time_bias, w, w_next, table, one_in, two_in, bias_in, small_sems, sems):
    small = [
        pltpu.make_async_copy(source, target, small_sems.at[i])
        for i, (source, target) in enumerate(((gain_one, one_in), (gain_two, two_in), (time_bias, bias_in)))
    ]
    copies = arranged(w_one, w, sems.at[0]) + arranged(w_two, w_next, sems.at[1])
    for copy in small + copies:
        copy.start()
    table[...] = jnp.zeros_like(table)
    for i, ref in enumerate((one_in, two_in, bias_in)):
        small[i].wait()
        table[i : i + 1] = ref[...].reshape(1, -1)
    for copy in copies:
        copy.wait()


def put_counts(ref, start, row):
    tail = ref.shape[0] - start
    room = ref.shape[1] - row.shape[1]
    wide = jnp.concatenate([row, jnp.zeros((1, room), F32)], axis=1)
    ref[start:] = jnp.broadcast_to(wide, (tail, ref.shape[1])).astype(BF16)


def get_counts(ref, start, columns):
    return ref[start : start + 8].astype(F32)[:1, :columns]


def by_column(values, anchor, columns):
    spot = lax.broadcasted_iota(jnp.int32, (columns, columns), 0) - anchor
    spot = jnp.where(spot < 0, spot + columns, spot)
    picked = spot == lax.broadcasted_iota(jnp.int32, (columns, columns), 1)
    return jnp.sum(jnp.where(picked, values, 0.0), axis=1, keepdims=True)


def first_kernel(size, mix, mix_other, full, full_other, edges, w, table, out, frame, acc, hidden):
    core = lax.axis_index("rows")
    rows, half_cols, channels = mix.shape
    columns, height, outs = 2 * half_cols, 2 * rows, out.shape[1] // 2
    count = height * columns * size
    summed = jnp.zeros((1, channels), F32)
    squares = jnp.zeros((1, channels), F32)
    for ref in (mix, mix_other, full, full_other):
        v = ref[...].astype(F32).reshape(rows * half_cols, channels)
        summed += jnp.sum(v, axis=0, keepdims=True)
        squares += jnp.sum(v * v, axis=0, keepdims=True)
    mean, scale = group_scale(summed, squares, count, size)
    scale = scale * table[0:1]
    frame[0] = jnp.zeros(frame.shape[1:], BF16)
    frame[height + 1] = jnp.zeros(frame.shape[1:], BF16)
    for ref, mine, col in ((mix, 0, 0), (full, 0, half_cols), (mix_other, 1, 0), (full_other, 1, half_cols)):
        start = 1 + rows * (core ^ mine)
        for row in range(rows):
            v = ref[row].astype(F32)
            frame[start + row, col : col + half_cols] = silu((v - mean) * scale).astype(BF16)
    nine_taps(frame, w, acc)
    bias = half_of(table[2:3], outs, core)
    summed = jnp.zeros((1, outs), F32)
    squares = jnp.zeros((1, outs), F32)
    for row in range(height):
        v = joined_taps(acc, row, columns, outs, edges) + bias
        hidden[row] = v
        summed += jnp.sum(v, axis=0, keepdims=True)
        squares += jnp.sum(v * v, axis=0, keepdims=True)
    mean, scale = group_scale(summed, squares, count, size)
    scale = scale * half_of(table[1:2], outs, core)
    for row in range(height):
        put(out, row, height, silu((hidden[row] - mean) * scale).astype(BF16))


def near_channels(outs):
    return outs // 128 * 128


def near_kernel(own, w, edges, part, frame, acc):
    core = lax.axis_index("rows")
    height, columns, near = frame.shape[0] - 2, frame.shape[1], frame.shape[2]
    outs = own.shape[1] // 2
    for edge in (0, height + 1):
        frame[edge] = jnp.zeros(frame.shape[1:], BF16)

    @pl.when(core == 0)
    def _():
        for row in range(height):
            frame[1 + row] = get(own, row, height, columns)[:, :near]

    @pl.when(core == 1)
    def _():
        for row in range(height):
            frame[1 + row] = get(own, row, height, columns)[:, outs - near :]

    nine_taps(frame, w, acc, core * (2 * outs - near))
    for row in range(height):
        part[row] = joined_taps(acc, row, columns, outs, edges)


def second_kernel(anchor_ref, own, other, w, edges, near_part, counts, load, mix_same, mix_cross, full_same, full_cross, frame, acc, result):
    core = lax.axis_index("rows")
    odd = (lax.axis_index("blk") & 1) == 1
    height, columns = frame.shape[0] - 2, frame.shape[1]
    outs = own.shape[1] // 2
    near = near_channels(outs)
    rows, half_cols = height // 2, columns // 2
    for edge in (0, height + 1):
        frame[edge] = jnp.zeros(frame.shape[1:], BF16)

    @pl.when(core == 0)
    def _():
        for row in range(height):
            mine, theirs = (get(ref, row, height, columns) for ref in (own, other))
            frame[1 + row] = jnp.concatenate([mine[:, near:], theirs], axis=1)

    @pl.when(core == 1)
    def _():
        for row in range(height):
            mine, theirs = (get(ref, row, height, columns) for ref in (own, other))
            frame[1 + row] = jnp.concatenate([theirs, mine[:, : outs - near]], axis=1)

    nine_taps(frame, w, acc, (1 - core) * near)
    own_row = jnp.where(odd, get_counts(load, rows * half_cols, columns), counts[...].astype(F32))
    part = jnp.broadcast_to(by_column(own_row, anchor_ref[0], columns), (columns, outs))
    for row in range(height):
        result[row] = (joined_taps(acc, row, columns, outs, edges) + near_part[row]) * part
    for out, flip, col in (
        (mix_same, 0, 0),
        (mix_cross, 1, 0),
        (full_same, 0, half_cols),
        (full_cross, 1, half_cols),
    ):
        start = rows * (core ^ flip)
        for row in range(rows):
            put(out, row, rows, result[start + row, col : col + half_cols].astype(BF16))
    for out in (mix_same, full_same):
        put_counts(out, rows * half_cols // 2, own_row)


def last_kernel(anchor_ref, latent, lowered, counts, load, mix_own, mix_core, mix_same, mix_cross, full_same, full_cross, out, done, sems):
    core = lax.axis_index("rows")
    odd = (lax.axis_index("blk") & 1) == 1
    anchor = anchor_ref[0]
    rows, cols, outs = latent.shape[0], latent.shape[1], latent.shape[2] // 2
    late = lax.broadcasted_iota(jnp.int32, (cols, outs), 0) >= anchor
    keep = late ^ odd
    tail = rows * cols // 2
    own_row = jnp.where(odd, get_counts(load, rows * cols, 2 * cols), counts[...].astype(F32))
    always = by_column(get_counts(full_same, tail, 2 * cols), anchor, 2 * cols)[cols:]
    ours = by_column(own_row, anchor, 2 * cols)[:cols]
    theirs = by_column(get_counts(mix_same, tail, 2 * cols), anchor, 2 * cols)[:cols]
    weight = always + jnp.where(keep[:, :1], ours, theirs)
    own_scale = math.sqrt(0.7 / 0.5)
    join_scale = math.sqrt(0.3) - math.sqrt(0.7 / 0.5) * math.sqrt(0.5)
    part = join_scale / weight

    copies = [pltpu.make_async_copy(done.at[row], out.at[row], sems.at[row]) for row in range(rows)]

    def summed(row, own, far, full):
        own, far, full = (get(ref, row, rows, cols).astype(F32) for ref in (own, far, full))
        return jnp.where(keep, own, far) + full

    for row in range(rows):
        same = summed(row, mix_own, mix_same, full_same)
        cross = summed(row, mix_core, mix_cross, full_cross)
        base = own_scale * latent[row] + join_scale * lowered[row].astype(F32)

        @pl.when(core == 0)
        def _():
            done[row] = base + part * jnp.concatenate([same, cross], axis=1)

        @pl.when(core == 1)
        def _():
            done[row] = base + part * jnp.concatenate([cross, same], axis=1)

        copies[row].start()
    for copy in copies:
        copy.wait()


def in_hbm(value):
    return pltpu.with_memory_space_constraint(value, pltpu.HBM)


def per_device(latent, offset, counts, conv_one, conv_two, gain_one, gain_two, time_bias):
    rows, stride, channels = latent.shape
    outs = conv_one.shape[3]
    size = channels // GROUPS
    height, columns = 2 * rows, 2 * stride
    odd = (lax.axis_index("blk") & 1) == 1
    anchor = offset[0]

    conv_one, conv_two = (jnp.swapaxes(v, 2, 3) for v in (conv_one, conv_two))
    lowered, load, held, counted = pl.pallas_call(
        lower_kernel,
        out_shape=(
            jax.ShapeDtypeStruct(latent.shape, BF16),
            jax.ShapeDtypeStruct((rows * stride + TAIL, channels), BF16),
            jax.ShapeDtypeStruct(latent.shape, F32),
            jax.ShapeDtypeStruct(counts.shape, counts.dtype),
        ),
        in_specs=[HBM] * 2,
        out_specs=(VMEM,) * 4,
        scratch_shapes=[pltpu.SemaphoreType.DMA((rows + 1,))],
        compiler_params=PARAMS,
    )(in_hbm(latent), in_hbm(counts))
    weights = jax.ShapeDtypeStruct((3, 3 * outs, channels), BF16)
    vector = pltpu.VMEM((channels,), F32)
    w_first, w_next, table = pl.pallas_call(
        ready_kernel,
        out_shape=(weights, weights, jax.ShapeDtypeStruct((8, channels), F32)),
        in_specs=[HBM] * 5,
        out_specs=(VMEM,) * 3,
        scratch_shapes=[vector] * 3 + [pltpu.SemaphoreType.DMA((3,)), pltpu.SemaphoreType.DMA((2, 18))],
        compiler_params=PARAMS,
    )(*[in_hbm(v) for v in (conv_one, conv_two, gain_one, gain_two, time_bias)])
    full = moved(lowered, lambda b: b ^ 1, 0)
    load = moved(load, lambda b: b + 2 if b % 2 else b - 2, 0)
    beyond = load[: rows * stride].reshape(latent.shape)
    spot = lax.broadcasted_iota(jnp.int32, (3, columns, 128), 1)
    kind = lax.broadcasted_iota(jnp.int32, (3, columns, 128), 0)
    cut = jnp.where(kind == 0, spot == anchor, spot == jnp.where(anchor == 0, columns, anchor) - 1)
    edges = jnp.where(jnp.where(kind == 2, spot < anchor, cut), 0.0, 1.0)

    full_other = moved(full, lambda b: b, 1)
    col = lax.broadcasted_iota(jnp.int32, lowered.shape, 1)
    mix = jnp.where((col >= anchor) ^ odd, lowered, beyond)
    mix_other = moved(mix, lambda b: b, 1)

    frame = pltpu.VMEM((height + 2, columns, channels), BF16)
    acc = pltpu.VMEM((height * columns, 3 * outs), F32)
    result = pltpu.VMEM((height, columns, outs), F32)
    own = pl.pallas_call(
        functools.partial(first_kernel, size),
        out_shape=packed(height, columns, outs),
        in_specs=[VMEM] * 7,
        out_specs=VMEM,
        scratch_shapes=[frame, acc, result],
        compiler_params=PARAMS,
    )(mix, mix_other, full, full_other, edges, w_first, table)
    other = moved(own, lambda b: b, 1)
    near = near_channels(outs)
    near_part = pl.pallas_call(
        near_kernel,
        out_shape=jax.ShapeDtypeStruct((height, columns, outs), F32),
        in_specs=[VMEM] * 3,
        out_specs=VMEM,
        scratch_shapes=[pltpu.VMEM((height + 2, columns, near), BF16), acc],
        compiler_params=PARAMS,
    )(own, w_next, edges)
    marked, plain = packed(rows, stride, outs, TAIL), packed(rows, stride, outs)
    mix_same, mix_cross, full_same, full_cross = pl.pallas_call(
        second_kernel,
        out_shape=(marked, plain, marked, plain),
        in_specs=[SMEM] + [VMEM] * 7,
        out_specs=(VMEM,) * 4,
        scratch_shapes=[pltpu.VMEM((height + 2, columns, channels - near), BF16), acc, result],
        compiler_params=PARAMS,
    )(offset, own, other, w_next, edges, near_part, counted, load)

    def aside(b):
        return b - 2 if b % 2 else b + 2

    got_mix_same = moved(mix_same, aside, 0)
    got_mix_cross = moved(mix_cross, aside, 1)
    got_full_same = moved(full_same, lambda b: b ^ 1, 0)
    got_full_cross = moved(full_cross, lambda b: b ^ 1, 1)
    got_core = moved(mix_cross, lambda b: b, 1)
    return pl.pallas_call(
        last_kernel,
        out_shape=jax.ShapeDtypeStruct(latent.shape, F32),
        in_specs=[SMEM] + [VMEM] * 10,
        out_specs=HBM,
        scratch_shapes=[pltpu.VMEM(latent.shape, F32), pltpu.SemaphoreType.DMA((rows,))],
        compiler_params=PARAMS,
    )(offset, held, lowered, counted, load, mix_same, got_core, got_mix_same, got_mix_cross, got_full_same, got_full_cross)


def solution(mesh):
    return jax.shard_map(
        per_device,
        mesh=mesh,
        in_specs=(
            P(("pano", "rows"), "blk", None),
            P("pano"),
            P(("pano", "blk"), None),
            P(None, None, None, "rows"),
            P(None, None, None, "rows"),
            P(),
            P(),
            P(),
        ),
        out_specs=P(("pano", "rows"), "blk", None),
        check_vma=False,
    )
```

```python
import functools
import math

import jax
import jax.numpy as jnp
from jax import lax
from jax.experimental import pallas as pl
from jax.experimental.pallas import tpu as pltpu
from jax.sharding import PartitionSpec as P

GROUPS = 32
PARAMS = pltpu.CompilerParams(vmem_limit_bytes=20 * 2**20)
VMEM = pl.BlockSpec(memory_space=pltpu.VMEM)
HBM = pl.BlockSpec(memory_space=pltpu.HBM)
SMEM = pl.BlockSpec(memory_space=pltpu.SMEM)
F32 = jnp.float32
BF16 = jnp.bfloat16


def moved(value, step, flip):
    blocks, cores = lax.axis_size("blk"), lax.axis_size("rows")
    pairs = [
        (b * cores + r, (step(b) % blocks) * cores + (r ^ flip))
        for b in range(blocks)
        for r in range(cores)
    ]
    return lax.ppermute(value, ("blk", "rows"), pairs)


def split3(x):
    high = x.astype(BF16)
    rest = x - high.astype(F32)
    mid = rest.astype(BF16)
    low = (rest - mid.astype(F32)).astype(BF16)
    return [high.astype(F32), mid.astype(F32), low.astype(F32)]


def regroup(first, second, table):
    rows = jnp.concatenate(split3(first) + split3(second) + [jnp.zeros_like(first)] * 2, axis=0)
    out = jnp.dot(rows.astype(BF16), table, preferred_element_type=F32)
    return out[0:1] + out[1:2] + out[2:3], out[3:4] + out[4:5] + out[5:6]


def group_tables(size, gather, spread):
    for ref, (ch_axis, group_axis) in ((gather, (0, 1)), (spread, (1, 0))):
        ch = lax.broadcasted_iota(jnp.int32, ref.shape, ch_axis)
        low = lax.broadcasted_iota(jnp.int32, ref.shape, group_axis) * size
        ref[...] = jnp.where((ch >= low) & (ch < low + size), 1.0, 0.0).astype(BF16)


def group_scale(summed, squares, count, gather, spread):
    channels = summed.shape[1]
    total, total_sq = regroup(summed, squares, gather[:channels])
    mean = total / count
    scale = lax.rsqrt(total_sq / count - mean * mean + 1e-05)
    return regroup(mean, scale, spread[:, :channels])


def silu_of_twice(half):
    return half + half * jnp.tanh(half)


def arranged(core, weight, target, sem):
    outs = weight.shape[2]
    whole = outs // 128 * 128
    copies, start = [], 0
    for part in (slice(0, whole), slice(whole, outs)):
        for b in range(3):
            size = part.stop - part.start
            for a in range(3):
                spot = target.at[a, start : start + size]
                tap = a + core * (2 - 2 * a)
                copies.append(pltpu.make_async_copy(weight.at[tap, b, part], spot, sem.at[len(copies)]))
            start += size
    return copies


def nine_taps(frame, weight, acc, channel=None):
    height, columns, channels = frame.shape[0] - 2, frame.shape[1], frame.shape[2]
    patch = jnp.concatenate(
        [frame[a : a + height].reshape(height * columns, channels) for a in range(3)], axis=1
    )
    some = slice(None) if channel is None else pl.ds(pl.multiple_of(channel, 128), channels)
    taps = jnp.concatenate([weight[a, :, some] for a in range(3)], axis=1)
    acc[...] = lax.dot_general(patch, taps, (((1,), (1,)), ((), ())), preferred_element_type=F32)


def clear_edges(frame):
    for edge in (0, frame.shape[0] - 1):
        frame[edge] = jnp.zeros(frame.shape[1:], BF16)


def local_row(core, i, rows):
    return i + core * (rows - 1 - 2 * i)


def joined_taps(acc, row, columns, outs, edges):
    block = acc[row * columns : (row + 1) * columns]
    whole = outs // 128 * 128

    def joined(start, width):
        first, second, third = (block[:, start + b * width : start + (b + 1) * width] for b in range(3))
        cuts = [jnp.concatenate([edges[b]] * pl.cdiv(width, 128), axis=1)[:, :width] for b in range(2)]
        return second + pltpu.roll(first, 1, 0) * cuts[0] + pltpu.roll(third, columns - 1, 0) * cuts[1]

    return jnp.concatenate([joined(0, whole), joined(3 * whole, outs - whole)], axis=1)


TAIL = 8


def packed(rows, columns, outs, tail=0):
    return jax.ShapeDtypeStruct((rows * columns // 2 + tail, 2 * outs), BF16)


def put(ref, row, rows, value):
    half, outs, columns = rows // 2, ref.shape[1] // 2, value.shape[0]
    spot = (row % half) * columns
    ref[spot : spot + columns, (row // half) * outs : (row // half + 1) * outs] = value


def get(ref, row, rows, columns):
    half, outs = rows // 2, ref.shape[1] // 2
    spot = (row % half) * columns
    return ref[spot : spot + columns, (row // half) * outs : (row // half + 1) * outs]


def half_of(row, outs, core):
    return jnp.where(core == 0, row[:, :outs], row[:, outs:])


def lower_kernel(latent, counts, lowered, load, held, counted, sems):
    rows, cols, _ = latent.shape
    copies = [pltpu.make_async_copy(latent.at[row], held.at[row], sems.at[row]) for row in range(rows)]
    copies.append(pltpu.make_async_copy(counts, counted, sems.at[rows]))
    for copy in copies:
        copy.start()
    for row in range(rows):
        copies[row].wait()
        value = held[row].astype(BF16)
        lowered[row] = value
        load[row * cols : (row + 1) * cols] = value
    copies[rows].wait()
    put_counts(load, rows * cols, counted[...].astype(F32))


def ready_kernel(size, w_one, w_two, gain_one, gain_two, time_bias, w, w_next, table, gather, spread, one_in, two_in, bias_in, small_sems, sems):
    small = [
        pltpu.make_async_copy(source, target, small_sems.at[i])
        for i, (source, target) in enumerate(((gain_one, one_in), (gain_two, two_in), (time_bias, bias_in)))
    ]
    core = lax.axis_index("rows")
    copies = arranged(core, w_one, w, sems.at[0]) + arranged(core, w_two, w_next, sems.at[1])
    for copy in small + copies:
        copy.start()
    group_tables(size, gather, spread)
    table[...] = jnp.zeros_like(table)
    for i, ref in enumerate((one_in, two_in, bias_in)):
        small[i].wait()
        table[i : i + 1] = ref[...].reshape(1, -1)
    for copy in copies:
        copy.wait()


def put_counts(ref, start, row):
    tail = ref.shape[0] - start
    room = ref.shape[1] - row.shape[1]
    wide = jnp.concatenate([row, jnp.zeros((1, room), F32)], axis=1)
    ref[start:] = jnp.broadcast_to(wide, (tail, ref.shape[1])).astype(BF16)


def get_counts(ref, start, columns):
    return ref[start : start + 8].astype(F32)[:1, :columns]


def by_column(values, anchor, columns):
    spot = lax.broadcasted_iota(jnp.int32, (columns, columns), 0) - anchor
    spot = jnp.where(spot < 0, spot + columns, spot)
    picked = spot == lax.broadcasted_iota(jnp.int32, (columns, columns), 1)
    return jnp.sum(jnp.where(picked, values, 0.0), axis=1, keepdims=True)


def first_kernel(size, mix, mix_other, full, full_other, edges, w, table, gather, spread, out, frame, acc, hidden):
    core = lax.axis_index("rows")
    rows, half_cols, channels = mix.shape
    columns, height, outs = 2 * half_cols, 2 * rows, out.shape[1] // 2
    count = height * columns * size
    clear_edges(frame)
    summed = jnp.zeros((1, channels), F32)
    squares = jnp.zeros((1, channels), F32)
    for ref in (mix, mix_other, full, full_other):
        v = ref[...].astype(F32).reshape(rows * half_cols, channels)
        summed += jnp.sum(v, axis=0, keepdims=True)
        squares += jnp.sum(v * v, axis=0, keepdims=True)
    mean, scale = group_scale(summed, squares, count, gather, spread)
    scale = scale * (0.5 * table[0:1])

    def normed(row):
        local = local_row(core, row % rows, rows)
        for ref, col in ((mix, 0), (full, half_cols)) if row < rows else ((mix_other, 0), (full_other, half_cols)):
            v = ref[local].astype(F32)
            frame[1 + row, col : col + half_cols] = silu_of_twice((v - mean) * scale).astype(BF16)

    for row in range(height):
        normed(row)
    nine_taps(frame, w, acc)
    bias = half_of(table[2:3], outs, core)
    summed = jnp.zeros((1, outs), F32)
    squares = jnp.zeros((1, outs), F32)
    for row in range(height):
        v = joined_taps(acc, row, columns, outs, edges) + bias
        hidden[row] = v
        summed += jnp.sum(v, axis=0, keepdims=True)
        squares += jnp.sum(v * v, axis=0, keepdims=True)
    mean, scale = group_scale(summed, squares, count, gather, spread)
    scale = scale * (0.5 * half_of(table[1:2], outs, core))
    for row in range(height):
        put(out, row, height, silu_of_twice((hidden[row] - mean) * scale).astype(BF16))


def near_channels(outs):
    return outs // 128 * 128


def near_kernel(own, w, edges, part, frame, acc):
    core = lax.axis_index("rows")
    height, columns, near = frame.shape[0] - 2, frame.shape[1], frame.shape[2]
    outs = own.shape[1] // 2
    clear_edges(frame)
    for row in range(height):
        mine = get(own, row, height, columns)
        frame[1 + row] = jnp.where(core == 0, mine[:, :near], mine[:, outs - near :])
    nine_taps(frame, w, acc, core * (2 * outs - near))
    for row in range(height):
        part[row] = joined_taps(acc, row, columns, outs, edges)


def second_kernel(anchor_ref, own, other, w, edges, near_part, counts, load, mix_same, mix_cross, full_same, full_cross, frame, acc):
    core = lax.axis_index("rows")
    odd = (lax.axis_index("blk") & 1) == 1
    height, columns = frame.shape[0] - 2, frame.shape[1]
    outs = own.shape[1] // 2
    near = near_channels(outs)
    rows, half_cols = height // 2, columns // 2
    clear_edges(frame)
    for row in range(height):
        mine = get(own, row, height, columns)
        theirs = get(other, height - 1 - row, height, columns)
        frame[1 + row] = jnp.where(
            core == 0,
            jnp.concatenate([mine[:, near:], theirs], axis=1),
            jnp.concatenate([theirs, mine[:, : outs - near]], axis=1),
        )
    nine_taps(frame, w, acc, (1 - core) * near)
    own_row = jnp.where(odd, get_counts(load, rows * half_cols, columns), counts[...].astype(F32))
    part = jnp.broadcast_to(by_column(own_row, anchor_ref[0], columns), (columns, outs))
    for row in range(height):
        value = ((joined_taps(acc, row, columns, outs, edges) + near_part[row]) * part).astype(BF16)
        mix, full = (mix_same, full_same) if row < rows else (mix_cross, full_cross)
        spot = row if row < rows else height - 1 - row
        put(mix, spot, rows, value[:half_cols])
        put(full, spot, rows, value[half_cols:])
    for out in (mix_same, full_same):
        put_counts(out, rows * half_cols // 2, own_row)


def last_kernel(anchor_ref, latent, lowered, counts, load, mix_own, mix_core, mix_same, mix_cross, full_same, full_cross, out, done, sems):
    core = lax.axis_index("rows")
    odd = (lax.axis_index("blk") & 1) == 1
    anchor = anchor_ref[0]
    rows, cols, outs = latent.shape[0], latent.shape[1], latent.shape[2] // 2
    late = lax.broadcasted_iota(jnp.int32, (cols, outs), 0) >= anchor
    keep = late ^ odd
    tail = rows * cols // 2
    own_row = jnp.where(odd, get_counts(load, rows * cols, 2 * cols), counts[...].astype(F32))
    always = by_column(get_counts(full_same, tail, 2 * cols), anchor, 2 * cols)[cols:]
    ours = by_column(own_row, anchor, 2 * cols)[:cols]
    theirs = by_column(get_counts(mix_same, tail, 2 * cols), anchor, 2 * cols)[:cols]
    weight = always + jnp.where(keep[:, :1], ours, theirs)
    own_scale = math.sqrt(0.7 / 0.5)
    join_scale = math.sqrt(0.3) - math.sqrt(0.7 / 0.5) * math.sqrt(0.5)
    part = join_scale / weight

    def summed(row, own, far, full):
        own, far, full = (get(ref, row, rows, cols).astype(F32) for ref in (own, far, full))
        return jnp.where(keep, own, far) + full

    copies = []
    for row in range(rows):
        local = local_row(core, row, rows)
        same = summed(row, mix_own, mix_same, full_same)
        cross = summed(row, mix_core, mix_cross, full_cross)
        base = own_scale * latent[local] + join_scale * lowered[local].astype(F32)
        both = jnp.where(
            core == 0, jnp.concatenate([same, cross], axis=1), jnp.concatenate([cross, same], axis=1)
        )
        done[row] = base + part * both
        copies.append(pltpu.make_async_copy(done.at[row], out.at[local], sems.at[row]))
        copies[row].start()
    for copy in copies:
        copy.wait()


def in_hbm(value):
    return pltpu.with_memory_space_constraint(value, pltpu.HBM)


def per_device(latent, offset, counts, conv_one, conv_two, gain_one, gain_two, time_bias):
    rows, stride, channels = latent.shape
    outs = conv_one.shape[3]
    size = channels // GROUPS
    height, columns = 2 * rows, 2 * stride
    odd = (lax.axis_index("blk") & 1) == 1
    anchor = offset[0]

    conv_one, conv_two = (jnp.swapaxes(v, 2, 3) for v in (conv_one, conv_two))
    lowered, load, held, counted = pl.pallas_call(
        lower_kernel,
        out_shape=(
            jax.ShapeDtypeStruct(latent.shape, BF16),
            jax.ShapeDtypeStruct((rows * stride + TAIL, channels), BF16),
            jax.ShapeDtypeStruct(latent.shape, F32),
            jax.ShapeDtypeStruct(counts.shape, counts.dtype),
        ),
        in_specs=[HBM] * 2,
        out_specs=(VMEM,) * 4,
        scratch_shapes=[pltpu.SemaphoreType.DMA((rows + 1,))],
        compiler_params=PARAMS,
    )(in_hbm(latent), in_hbm(counts))
    weights = jax.ShapeDtypeStruct((3, 3 * outs, channels), BF16)
    vector = pltpu.VMEM((channels,), F32)
    w_first, w_next, table, gather, spread = pl.pallas_call(
        functools.partial(ready_kernel, size),
        out_shape=(
            weights,
            weights,
            jax.ShapeDtypeStruct((8, channels), F32),
            jax.ShapeDtypeStruct((channels, 128), BF16),
            jax.ShapeDtypeStruct((128, channels), BF16),
        ),
        in_specs=[HBM] * 5,
        out_specs=(VMEM,) * 5,
        scratch_shapes=[vector] * 3 + [pltpu.SemaphoreType.DMA((3,)), pltpu.SemaphoreType.DMA((2, 18))],
        compiler_params=PARAMS,
    )(*[in_hbm(v) for v in (conv_one, conv_two, gain_one, gain_two, time_bias)])
    full = moved(lowered, lambda b: b ^ 1, 0)
    load = moved(load, lambda b: b + 2 if b % 2 else b - 2, 0)
    beyond = load[: rows * stride].reshape(latent.shape)
    spot = lax.broadcasted_iota(jnp.int32, (3, columns, 128), 1)
    kind = lax.broadcasted_iota(jnp.int32, (3, columns, 128), 0)
    cut = jnp.where(kind == 0, spot == anchor, spot == jnp.where(anchor == 0, columns, anchor) - 1)
    edges = jnp.where(jnp.where(kind == 2, spot < anchor, cut), 0.0, 1.0)

    full_other = moved(full, lambda b: b, 1)
    col = lax.broadcasted_iota(jnp.int32, lowered.shape, 1)
    mix = jnp.where((col >= anchor) ^ odd, lowered, beyond)
    mix_other = moved(mix, lambda b: b, 1)

    frame = pltpu.VMEM((height + 2, columns, channels), BF16)
    acc = pltpu.VMEM((height * columns, 3 * outs), F32)
    result = pltpu.VMEM((height, columns, outs), F32)
    own = pl.pallas_call(
        functools.partial(first_kernel, size),
        out_shape=packed(height, columns, outs),
        in_specs=[VMEM] * 9,
        out_specs=VMEM,
        scratch_shapes=[frame, acc, result],
        compiler_params=PARAMS,
    )(mix, mix_other, full, full_other, edges, w_first, table, gather, spread)
    other = moved(own, lambda b: b, 1)
    near = near_channels(outs)
    near_part = pl.pallas_call(
        near_kernel,
        out_shape=jax.ShapeDtypeStruct((height, columns, outs), F32),
        in_specs=[VMEM] * 3,
        out_specs=VMEM,
        scratch_shapes=[pltpu.VMEM((height + 2, columns, near), BF16), acc],
        compiler_params=PARAMS,
    )(own, w_next, edges)
    marked, plain = packed(rows, stride, outs, TAIL), packed(rows, stride, outs)
    mix_same, mix_cross, full_same, full_cross = pl.pallas_call(
        second_kernel,
        out_shape=(marked, plain, marked, plain),
        in_specs=[SMEM] + [VMEM] * 7,
        out_specs=(VMEM,) * 4,
        scratch_shapes=[pltpu.VMEM((height + 2, columns, channels - near), BF16), acc],
        compiler_params=PARAMS,
    )(offset, own, other, w_next, edges, near_part, counted, load)

    def aside(b):
        return b - 2 if b % 2 else b + 2

    got_mix_same = moved(mix_same, aside, 0)
    got_mix_cross = moved(mix_cross, aside, 1)
    got_full_same = moved(full_same, lambda b: b ^ 1, 0)
    got_full_cross = moved(full_cross, lambda b: b ^ 1, 1)
    got_core = moved(mix_cross, lambda b: b, 1)
    return pl.pallas_call(
        last_kernel,
        out_shape=jax.ShapeDtypeStruct(latent.shape, F32),
        in_specs=[SMEM] + [VMEM] * 10,
        out_specs=HBM,
        scratch_shapes=[pltpu.VMEM(latent.shape, F32), pltpu.SemaphoreType.DMA((rows,))],
        compiler_params=PARAMS,
    )(offset, held, lowered, counted, load, mix_same, got_core, got_mix_same, got_mix_cross, got_full_same, got_full_cross)


def solution(mesh):
    return jax.shard_map(
        per_device,
        mesh=mesh,
        in_specs=(
            P(("pano", "rows"), "blk", None),
            P("pano"),
            P(("pano", "blk"), None),
            P(None, None, None, "rows"),
            P(None, None, None, "rows"),
            P(),
            P(),
            P(),
        ),
        out_specs=P(("pano", "rows"), "blk", None),
        check_vma=False,
    )
```

```python
import functools
import math

import jax
import jax.numpy as jnp
from jax import lax
from jax.experimental import pallas as pl
from jax.experimental.pallas import tpu as pltpu
from jax.sharding import PartitionSpec as P

GROUPS = 32
PARAMS = pltpu.CompilerParams(vmem_limit_bytes=20 * 2**20)
VMEM = pl.BlockSpec(memory_space=pltpu.VMEM)
HBM = pl.BlockSpec(memory_space=pltpu.HBM)
SMEM = pl.BlockSpec(memory_space=pltpu.SMEM)
F32 = jnp.float32
BF16 = jnp.bfloat16
OWN_SCALE = math.sqrt(0.7 / 0.5)
JOIN_SCALE = math.sqrt(0.3) - math.sqrt(0.7 / 0.5) * math.sqrt(0.5)


def moved(value, step, flip):
    blocks, cores = lax.axis_size("blk"), lax.axis_size("rows")
    pairs = [
        (b * cores + r, (step(b) % blocks) * cores + (r ^ flip))
        for b in range(blocks)
        for r in range(cores)
    ]
    return lax.ppermute(value, ("blk", "rows"), pairs)


def split3(x):
    high = x.astype(BF16)
    rest = x - high.astype(F32)
    mid = rest.astype(BF16)
    low = (rest - mid.astype(F32)).astype(BF16)
    return [high.astype(F32), mid.astype(F32), low.astype(F32)]


def regroup(first, second, table):
    rows = jnp.concatenate(split3(first) + split3(second) + [jnp.zeros_like(first)] * 2, axis=0)
    out = jnp.dot(rows.astype(BF16), table, preferred_element_type=F32)
    return out[0:1] + out[1:2] + out[2:3], out[3:4] + out[4:5] + out[5:6]


def group_tables(size, gather, spread):
    for ref, (ch_axis, group_axis) in ((gather, (0, 1)), (spread, (1, 0))):
        ch = lax.broadcasted_iota(jnp.int32, ref.shape, ch_axis)
        low = lax.broadcasted_iota(jnp.int32, ref.shape, group_axis) * size
        ref[...] = jnp.where((ch >= low) & (ch < low + size), 1.0, 0.0).astype(BF16)


def group_scale(summed, squares, count, gather, spread):
    channels = summed.shape[1]
    total, total_sq = regroup(summed, squares, gather[:channels])
    mean = total / count
    scale = lax.rsqrt(total_sq / count - mean * mean + 1e-05)
    return regroup(mean, scale, spread[:, :channels])


def silu_of_twice(half):
    return half + half * jnp.tanh(half)


def arranged(core, weight, target, sem):
    outs = weight.shape[2]
    whole = outs // 128 * 128
    copies, start = [], 0
    for part in (slice(0, whole), slice(whole, outs)):
        for b in range(3):
            size = part.stop - part.start
            for a in range(3):
                spot = target.at[a, start : start + size]
                tap = a + core * (2 - 2 * a)
                copies.append(pltpu.make_async_copy(weight.at[tap, b, part], spot, sem.at[len(copies)]))
            start += size
    return copies


def nine_taps(frame, weight, acc, channel=None):
    height, columns, channels = frame.shape[0] - 2, frame.shape[1], frame.shape[2]
    patch = jnp.concatenate(
        [frame[a : a + height].reshape(height * columns, channels) for a in range(3)], axis=1
    )
    some = slice(None) if channel is None else pl.ds(pl.multiple_of(channel, 128), channels)
    taps = jnp.concatenate([weight[a, :, some] for a in range(3)], axis=1)
    acc[...] = lax.dot_general(patch, taps, (((1,), (1,)), ((), ())), preferred_element_type=F32)


def clear_edges(frame):
    for edge in (0, frame.shape[0] - 1):
        frame[edge] = jnp.zeros(frame.shape[1:], BF16)


def local_row(core, i, rows):
    return i + core * (rows - 1 - 2 * i)


def joined_taps(acc, row, columns, outs, edges):
    block = acc[row * columns : (row + 1) * columns]
    whole = outs // 128 * 128

    def joined(start, width):
        first, second, third = (block[:, start + b * width : start + (b + 1) * width] for b in range(3))
        cuts = [jnp.concatenate([edges[b]] * pl.cdiv(width, 128), axis=1)[:, :width] for b in range(2)]
        return second + pltpu.roll(first, 1, 0) * cuts[0] + pltpu.roll(third, columns - 1, 0) * cuts[1]

    return jnp.concatenate([joined(0, whole), joined(3 * whole, outs - whole)], axis=1)


TAIL = 8


LANES = 128


def stacked(pixels, channels, tail=0):
    return jax.ShapeDtypeStruct((pixels * channels // LANES + tail, LANES), BF16)


def packed(rows, columns, outs, tail=0):
    return stacked(rows * columns // 2, 2 * outs, tail)


def spans(row, rows, columns, outs):
    half, whole = rows // 2, outs // LANES
    second, rest = row // half, outs % LANES
    tiles = [(second * (whole + 1) + t, 0, t * LANES, LANES) for t in range(whole)]
    tiles.append((whole, second * rest, whole * LANES, rest))
    start = (row % half) * columns
    return [
        (
            slice(tile * half * columns + start, tile * half * columns + start + columns),
            slice(lane, lane + size),
            slice(channel, channel + size),
        )
        for tile, lane, channel, size in tiles
    ]


def put(ref, row, rows, value):
    for place, lanes, part in spans(row, rows, *value.shape):
        ref[place, lanes] = value[:, part]


def get(ref, row, rows, columns, outs):
    return jnp.concatenate([ref[place, lanes] for place, lanes, _ in spans(row, rows, columns, outs)], axis=1)


def row_of(ref, row, rows, columns, channels):
    return jnp.concatenate(
        [
            ref[pl.ds(pl.multiple_of(t * rows * columns + row * columns, columns), columns)]
            for t in range(channels // LANES)
        ],
        axis=1,
    )


def half_of(row, outs, core):
    return jnp.where(core == 0, row[:, :outs], row[:, outs:])


def lower_kernel(latent, counts, lowered, load, held, counted, sems):
    rows, cols, channels = latent.shape
    copies = [pltpu.make_async_copy(latent.at[row], held.at[row], sems.at[row]) for row in range(rows)]
    copies.append(pltpu.make_async_copy(counts, counted, sems.at[rows]))
    for copy in copies:
        copy.start()
    for row in range(rows):
        copies[row].wait()
        value = held[row].astype(BF16)
        for t in range(channels // LANES):
            start = t * rows * cols + row * cols
            for ref in (lowered, load):
                ref[start : start + cols] = value[:, t * LANES : (t + 1) * LANES]
    copies[rows].wait()
    put_counts(load, counted[...].astype(F32))


def ready_kernel(size, held, w_one, w_two, gain_one, gain_two, time_bias, w, w_next, table, gather, spread, base, one_in, two_in, bias_in, small_sems, sems):
    small = [
        pltpu.make_async_copy(source, target, small_sems.at[i])
        for i, (source, target) in enumerate(((gain_one, one_in), (gain_two, two_in), (time_bias, bias_in)))
    ]
    core = lax.axis_index("rows")
    copies = arranged(core, w_one, w, sems.at[0]) + arranged(core, w_two, w_next, sems.at[1])
    for copy in small + copies:
        copy.start()
    group_tables(size, gather, spread)
    for row in range(held.shape[0]):
        value = held[local_row(core, row, held.shape[0])]
        base[row] = OWN_SCALE * value + JOIN_SCALE * value.astype(BF16).astype(F32)
    table[...] = jnp.zeros_like(table)
    for i, ref in enumerate((one_in, two_in, bias_in)):
        small[i].wait()
        table[i : i + 1] = ref[...].reshape(1, -1)
    for copy in copies:
        copy.wait()


def put_counts(ref, row):
    wide = jnp.concatenate([row, jnp.zeros((1, LANES - row.shape[1]), F32)], axis=1)
    ref[ref.shape[0] - TAIL :] = jnp.broadcast_to(wide, (TAIL, LANES)).astype(BF16)


def get_counts(ref, columns):
    return ref[ref.shape[0] - TAIL :].astype(F32)[:1, :columns]


def by_column(values, anchor, columns):
    spot = lax.broadcasted_iota(jnp.int32, (columns, columns), 0) - anchor
    spot = jnp.where(spot < 0, spot + columns, spot)
    picked = spot == lax.broadcasted_iota(jnp.int32, (columns, columns), 1)
    return jnp.sum(jnp.where(picked, values, 0.0), axis=1, keepdims=True)


def first_kernel(size, rows, mix, mix_other, full, full_other, edges, w, table, gather, spread, out, frame, acc, hidden):
    core = lax.axis_index("rows")
    height, columns, outs = hidden.shape
    half_cols, channels = columns // 2, frame.shape[2]
    count = height * columns * size
    clear_edges(frame)
    summed = jnp.zeros((1, channels), F32)
    squares = jnp.zeros((1, channels), F32)
    for ref in (mix, mix_other, full, full_other):
        v = row_of(ref, 0, 1, rows * half_cols, channels).astype(F32)
        summed += jnp.sum(v, axis=0, keepdims=True)
        squares += jnp.sum(v * v, axis=0, keepdims=True)
    mean, scale = group_scale(summed, squares, count, gather, spread)
    scale = scale * (0.5 * table[0:1])

    def normed(row):
        local = local_row(core, row % rows, rows)
        for ref, col in ((mix, 0), (full, half_cols)) if row < rows else ((mix_other, 0), (full_other, half_cols)):
            v = row_of(ref, local, rows, half_cols, channels).astype(F32)
            frame[1 + row, col : col + half_cols] = silu_of_twice((v - mean) * scale).astype(BF16)

    for row in range(height):
        normed(row)
    nine_taps(frame, w, acc)
    bias = half_of(table[2:3], outs, core)
    summed = jnp.zeros((1, outs), F32)
    squares = jnp.zeros((1, outs), F32)
    for row in range(height):
        v = joined_taps(acc, row, columns, outs, edges) + bias
        hidden[row] = v
        summed += jnp.sum(v, axis=0, keepdims=True)
        squares += jnp.sum(v * v, axis=0, keepdims=True)
    mean, scale = group_scale(summed, squares, count, gather, spread)
    scale = scale * (0.5 * half_of(table[1:2], outs, core))
    for row in range(height):
        put(out, row, height, silu_of_twice((hidden[row] - mean) * scale).astype(BF16))


def near_channels(outs):
    return outs // 128 * 128


def near_kernel(own, w, edges, part, frame, acc):
    core = lax.axis_index("rows")
    height, columns, near = frame.shape[0] - 2, frame.shape[1], frame.shape[2]
    outs = part.shape[2]
    clear_edges(frame)
    for row in range(height):
        mine = get(own, row, height, columns, outs)
        frame[1 + row] = jnp.where(core == 0, mine[:, :near], mine[:, outs - near :])
    nine_taps(frame, w, acc, core * (2 * outs - near))
    for row in range(height):
        part[row] = joined_taps(acc, row, columns, outs, edges)


def second_kernel(anchor_ref, own, other, w, edges, near_part, counts, load, mix_same, mix_cross, full_same, full_cross, frame, acc):
    core = lax.axis_index("rows")
    odd = (lax.axis_index("blk") & 1) == 1
    height, columns = frame.shape[0] - 2, frame.shape[1]
    outs = near_part.shape[2]
    near = near_channels(outs)
    rows, half_cols = height // 2, columns // 2
    clear_edges(frame)
    for row in range(height):
        mine = get(own, row, height, columns, outs)
        theirs = get(other, height - 1 - row, height, columns, outs)
        frame[1 + row] = jnp.where(
            core == 0,
            jnp.concatenate([mine[:, near:], theirs], axis=1),
            jnp.concatenate([theirs, mine[:, : outs - near]], axis=1),
        )
    nine_taps(frame, w, acc, (1 - core) * near)
    own_row = jnp.where(odd, get_counts(load, columns), counts[...].astype(F32))
    part = jnp.broadcast_to(by_column(own_row, anchor_ref[0], columns), (columns, outs))
    for row in range(height):
        value = ((joined_taps(acc, row, columns, outs, edges) + near_part[row]) * part).astype(BF16)
        mix, full = (mix_same, full_same) if row < rows else (mix_cross, full_cross)
        spot = row if row < rows else height - 1 - row
        put(mix, spot, rows, value[:half_cols])
        put(full, spot, rows, value[half_cols:])
    for out in (mix_same, full_same):
        put_counts(out, own_row)


def last_kernel(anchor_ref, base, counts, load, mix_own, mix_core, mix_same, mix_cross, full_same, full_cross, out, done, sems):
    core = lax.axis_index("rows")
    odd = (lax.axis_index("blk") & 1) == 1
    anchor = anchor_ref[0]
    rows, cols, outs = base.shape[0], base.shape[1], base.shape[2] // 2
    late = lax.broadcasted_iota(jnp.int32, (cols, outs), 0) >= anchor
    keep = late ^ odd
    own_row = jnp.where(odd, get_counts(load, 2 * cols), counts[...].astype(F32))
    always = by_column(get_counts(full_same, 2 * cols), anchor, 2 * cols)[cols:]
    ours = by_column(own_row, anchor, 2 * cols)[:cols]
    theirs = by_column(get_counts(mix_same, 2 * cols), anchor, 2 * cols)[:cols]
    weight = always + jnp.where(keep[:, :1], ours, theirs)
    part = JOIN_SCALE / weight

    def summed(row, own, far, full):
        own, far, full = (get(ref, row, rows, cols, outs).astype(F32) for ref in (own, far, full))
        return jnp.where(keep, own, far) + full

    copies = []
    for row in range(rows):
        local = local_row(core, row, rows)
        same = summed(row, mix_own, mix_same, full_same)
        cross = summed(row, mix_core, mix_cross, full_cross)
        both = jnp.where(
            core == 0, jnp.concatenate([same, cross], axis=1), jnp.concatenate([cross, same], axis=1)
        )
        done[row] = base[row] + part * both
        copies.append(pltpu.make_async_copy(done.at[row], out.at[local], sems.at[row]))
        copies[row].start()
    for copy in copies:
        copy.wait()


def in_hbm(value):
    return pltpu.with_memory_space_constraint(value, pltpu.HBM)


def per_device(latent, offset, counts, conv_one, conv_two, gain_one, gain_two, time_bias):
    rows, stride, channels = latent.shape
    outs = conv_one.shape[3]
    size = channels // GROUPS
    height, columns = 2 * rows, 2 * stride
    odd = (lax.axis_index("blk") & 1) == 1
    anchor = offset[0]

    conv_one, conv_two = (jnp.swapaxes(v, 2, 3) for v in (conv_one, conv_two))
    lowered, load, held, counted = pl.pallas_call(
        lower_kernel,
        out_shape=(
            stacked(rows * stride, channels),
            stacked(rows * stride, channels, TAIL),
            jax.ShapeDtypeStruct(latent.shape, F32),
            jax.ShapeDtypeStruct(counts.shape, counts.dtype),
        ),
        in_specs=[HBM] * 2,
        out_specs=(VMEM,) * 4,
        scratch_shapes=[pltpu.SemaphoreType.DMA((rows + 1,))],
        compiler_params=PARAMS,
    )(in_hbm(latent), in_hbm(counts))
    weights = jax.ShapeDtypeStruct((3, 3 * outs, channels), BF16)
    vector = pltpu.VMEM((channels,), F32)
    w_first, w_next, table, gather, spread, base = pl.pallas_call(
        functools.partial(ready_kernel, size),
        out_shape=(
            weights,
            weights,
            jax.ShapeDtypeStruct((8, channels), F32),
            jax.ShapeDtypeStruct((channels, 128), BF16),
            jax.ShapeDtypeStruct((128, channels), BF16),
            jax.ShapeDtypeStruct(latent.shape, F32),
        ),
        in_specs=[VMEM] + [HBM] * 5,
        out_specs=(VMEM,) * 6,
        scratch_shapes=[vector] * 3 + [pltpu.SemaphoreType.DMA((3,)), pltpu.SemaphoreType.DMA((2, 18))],
        compiler_params=PARAMS,
    )(held, *[in_hbm(v) for v in (conv_one, conv_two, gain_one, gain_two, time_bias)])
    full = moved(lowered, lambda b: b ^ 1, 0)
    load = moved(load, lambda b: b + 2 if b % 2 else b - 2, 0)
    beyond = load[: lowered.shape[0]]
    blocks = (-1, stride, LANES)
    spot = lax.broadcasted_iota(jnp.int32, (3, columns, 128), 1)
    kind = lax.broadcasted_iota(jnp.int32, (3, columns, 128), 0)
    cut = jnp.where(kind == 0, spot == anchor, spot == jnp.where(anchor == 0, columns, anchor) - 1)
    edges = jnp.where(jnp.where(kind == 2, spot < anchor, cut), 0.0, 1.0)

    full_other = moved(full, lambda b: b, 1)
    lowered_blocks, beyond = lowered.reshape(blocks), beyond.reshape(blocks)
    col = lax.broadcasted_iota(jnp.int32, beyond.shape, 1)
    mix = jnp.where((col >= anchor) ^ odd, lowered_blocks, beyond).reshape(lowered.shape)
    mix_other = moved(mix, lambda b: b, 1)

    frame = pltpu.VMEM((height + 2, columns, channels), BF16)
    acc = pltpu.VMEM((height * columns, 3 * outs), F32)
    result = pltpu.VMEM((height, columns, outs), F32)
    own = pl.pallas_call(
        functools.partial(first_kernel, size, rows),
        out_shape=packed(height, columns, outs),
        in_specs=[VMEM] * 9,
        out_specs=VMEM,
        scratch_shapes=[frame, acc, result],
        compiler_params=PARAMS,
    )(mix, mix_other, full, full_other, edges, w_first, table, gather, spread)
    other = moved(own, lambda b: b, 1)
    near = near_channels(outs)
    near_part = pl.pallas_call(
        near_kernel,
        out_shape=jax.ShapeDtypeStruct((height, columns, outs), F32),
        in_specs=[VMEM] * 3,
        out_specs=VMEM,
        scratch_shapes=[pltpu.VMEM((height + 2, columns, near), BF16), acc],
        compiler_params=PARAMS,
    )(own, w_next, edges)
    marked, plain = packed(rows, stride, outs, TAIL), packed(rows, stride, outs)
    mix_same, mix_cross, full_same, full_cross = pl.pallas_call(
        second_kernel,
        out_shape=(marked, plain, marked, plain),
        in_specs=[SMEM] + [VMEM] * 7,
        out_specs=(VMEM,) * 4,
        scratch_shapes=[pltpu.VMEM((height + 2, columns, channels - near), BF16), acc],
        compiler_params=PARAMS,
    )(offset, own, other, w_next, edges, near_part, counted, load)

    def aside(b):
        return b - 2 if b % 2 else b + 2

    got_mix_same = moved(mix_same, aside, 0)
    got_mix_cross = moved(mix_cross, aside, 1)
    got_full_same = moved(full_same, lambda b: b ^ 1, 0)
    got_full_cross = moved(full_cross, lambda b: b ^ 1, 1)
    got_core = moved(mix_cross, lambda b: b, 1)
    return pl.pallas_call(
        last_kernel,
        out_shape=jax.ShapeDtypeStruct(latent.shape, F32),
        in_specs=[SMEM] + [VMEM] * 9,
        out_specs=HBM,
        scratch_shapes=[pltpu.VMEM(latent.shape, F32), pltpu.SemaphoreType.DMA((rows,))],
        compiler_params=PARAMS,
    )(offset, base, counted, load, mix_same, got_core, got_mix_same, got_mix_cross, got_full_same, got_full_cross)


def solution(mesh):
    return jax.shard_map(
        per_device,
        mesh=mesh,
        in_specs=(
            P(("pano", "rows"), "blk", None),
            P("pano"),
            P(("pano", "blk"), None),
            P(None, None, None, "rows"),
            P(None, None, None, "rows"),
            P(),
            P(),
            P(),
        ),
        out_specs=P(("pano", "rows"), "blk", None),
        check_vma=False,
    )
```

```python
import functools
import math

import jax
import jax.numpy as jnp
from jax import lax
from jax.experimental import pallas as pl
from jax.experimental.pallas import tpu as pltpu
from jax.sharding import PartitionSpec as P

GROUPS = 32
PARAMS = pltpu.CompilerParams(vmem_limit_bytes=20 * 2**20)
VMEM = pl.BlockSpec(memory_space=pltpu.VMEM)
HBM = pl.BlockSpec(memory_space=pltpu.HBM)
SMEM = pl.BlockSpec(memory_space=pltpu.SMEM)
F32 = jnp.float32
BF16 = jnp.bfloat16
OWN_SCALE = math.sqrt(0.7 / 0.5)
JOIN_SCALE = math.sqrt(0.3) - math.sqrt(0.7 / 0.5) * math.sqrt(0.5)


def moved(value, step, flip):
    blocks, cores = lax.axis_size("blk"), lax.axis_size("rows")
    pairs = [
        (b * cores + r, (step(b) % blocks) * cores + (r ^ flip))
        for b in range(blocks)
        for r in range(cores)
    ]
    return lax.ppermute(value, ("blk", "rows"), pairs)


def split3(x):
    high = x.astype(BF16)
    rest = x - high.astype(F32)
    mid = rest.astype(BF16)
    low = (rest - mid.astype(F32)).astype(BF16)
    return [high.astype(F32), mid.astype(F32), low.astype(F32)]


def regroup(first, second, table):
    rows = jnp.concatenate(split3(first) + split3(second) + [jnp.zeros_like(first)] * 2, axis=0)
    out = jnp.dot(rows.astype(BF16), table, preferred_element_type=F32)
    return out[0:1] + out[1:2] + out[2:3], out[3:4] + out[4:5] + out[5:6]


def group_tables(size, gather, spread):
    for ref, (ch_axis, group_axis) in ((gather, (0, 1)), (spread, (1, 0))):
        ch = lax.broadcasted_iota(jnp.int32, ref.shape, ch_axis)
        low = lax.broadcasted_iota(jnp.int32, ref.shape, group_axis) * size
        ref[...] = jnp.where((ch >= low) & (ch < low + size), 1.0, 0.0).astype(BF16)


def group_scale(summed, squares, count, gather, spread):
    channels = summed.shape[1]
    total, total_sq = regroup(summed, squares, gather[:channels])
    mean = total / count
    scale = lax.rsqrt(total_sq / count - mean * mean + 1e-05)
    return regroup(mean, scale, spread[:, :channels])


def silu_of_twice(half):
    return half + half * jnp.tanh(half)


def arranged(core, weight, target, sem):
    outs = weight.shape[2]
    whole = outs // 128 * 128
    copies, start = [], 0
    for part in (slice(0, whole), slice(whole, outs)):
        for b in range(3):
            size = part.stop - part.start
            for a in range(3):
                spot = target.at[a, start : start + size]
                tap = a + core * (2 - 2 * a)
                copies.append(pltpu.make_async_copy(weight.at[tap, b, part], spot, sem.at[len(copies)]))
            start += size
    return copies


def nine_taps(frame, weight, acc, channel=None):
    height, columns, channels = frame.shape[0] - 2, frame.shape[1], frame.shape[2]
    patch = jnp.concatenate(
        [frame[a : a + height].reshape(height * columns, channels) for a in range(3)], axis=1
    )
    some = slice(None) if channel is None else pl.ds(pl.multiple_of(channel, 128), channels)
    taps = jnp.concatenate([weight[a, :, some] for a in range(3)], axis=1)
    acc[...] = lax.dot_general(patch, taps, (((1,), (1,)), ((), ())), preferred_element_type=F32)


def clear_edges(frame):
    for edge in (0, frame.shape[0] - 1):
        frame[edge] = jnp.zeros(frame.shape[1:], BF16)


def local_row(core, i, rows):
    return i + core * (rows - 1 - 2 * i)


def joined_taps(acc, row, columns, outs, edges):
    block = acc[row * columns : (row + 1) * columns]
    whole = outs // 128 * 128

    def joined(start, width):
        first, second, third = (block[:, start + b * width : start + (b + 1) * width] for b in range(3))
        cuts = [jnp.concatenate([edges[b]] * pl.cdiv(width, 128), axis=1)[:, :width] for b in range(2)]
        return second + pltpu.roll(first, 1, 0) * cuts[0] + pltpu.roll(third, columns - 1, 0) * cuts[1]

    return jnp.concatenate([joined(0, whole), joined(3 * whole, outs - whole)], axis=1)


TAIL = 8


LANES = 128


def stacked(pixels, channels, tail=0):
    return jax.ShapeDtypeStruct((pixels * channels // LANES + tail, LANES), BF16)


def packed(rows, columns, outs, tail=0):
    return stacked(rows * columns // 2, 2 * outs, tail)


def spans(row, rows, columns, outs):
    half, whole = rows // 2, outs // LANES
    second, rest = row // half, outs % LANES
    tiles = [(second * (whole + 1) + t, 0, t * LANES, LANES) for t in range(whole)]
    tiles.append((whole, second * rest, whole * LANES, rest))
    start = (row % half) * columns
    return [
        (
            slice(tile * half * columns + start, tile * half * columns + start + columns),
            slice(lane, lane + size),
            slice(channel, channel + size),
        )
        for tile, lane, channel, size in tiles
    ]


def put(ref, row, rows, value):
    for place, lanes, part in spans(row, rows, *value.shape):
        ref[place, lanes] = value[:, part]


def get(ref, row, rows, columns, outs):
    return jnp.concatenate([ref[place, lanes] for place, lanes, _ in spans(row, rows, columns, outs)], axis=1)


def row_of(ref, row, rows, columns, channels):
    return jnp.concatenate(
        [
            ref[pl.ds(pl.multiple_of(t * rows * columns + row * columns, columns), columns)]
            for t in range(channels // LANES)
        ],
        axis=1,
    )


def half_of(row, outs, core):
    return jnp.where(core == 0, row[:, :outs], row[:, outs:])


def lower_kernel(latent, counts, lowered, load, held, counted, sems):
    rows, cols, channels = latent.shape
    copies = [pltpu.make_async_copy(latent.at[row], held.at[row], sems.at[row]) for row in range(rows)]
    copies.append(pltpu.make_async_copy(counts, counted, sems.at[rows]))
    for copy in copies:
        copy.start()
    for row in range(rows):
        copies[row].wait()
        value = held[row].astype(BF16)
        for t in range(channels // LANES):
            start = t * rows * cols + row * cols
            for ref in (lowered, load):
                ref[start : start + cols] = value[:, t * LANES : (t + 1) * LANES]
    copies[rows].wait()
    put_counts(load, counted[...].astype(F32))


def ready_kernel(size, anchor_ref, held, w_one, w_two, gain_one, gain_two, time_bias, w, w_next, table, gather, spread, base, edges, one_in, two_in, bias_in, small_sems, sems):
    small = [
        pltpu.make_async_copy(source, target, small_sems.at[i])
        for i, (source, target) in enumerate(((gain_one, one_in), (gain_two, two_in), (time_bias, bias_in)))
    ]
    core = lax.axis_index("rows")
    copies = arranged(core, w_one, w, sems.at[0]) + arranged(core, w_two, w_next, sems.at[1])
    for copy in small + copies:
        copy.start()
    group_tables(size, gather, spread)
    anchor, (columns, lanes) = anchor_ref[0], edges.shape[1:]
    col = lax.broadcasted_iota(jnp.int32, (columns, lanes), 0)
    for i, cut in enumerate((anchor, jnp.where(anchor == 0, columns, anchor) - 1)):
        edges[i] = jnp.where(col == cut, 0.0, 1.0)
    for row in range(held.shape[0]):
        value = held[local_row(core, row, held.shape[0])]
        base[row] = OWN_SCALE * value + JOIN_SCALE * value.astype(BF16).astype(F32)
    table[...] = jnp.zeros_like(table)
    for i, ref in enumerate((one_in, two_in, bias_in)):
        small[i].wait()
        table[i : i + 1] = ref[...].reshape(1, -1)
    for copy in copies:
        copy.wait()


def put_counts(ref, row):
    wide = jnp.concatenate([row, jnp.zeros((1, LANES - row.shape[1]), F32)], axis=1)
    ref[ref.shape[0] - TAIL :] = jnp.broadcast_to(wide, (TAIL, LANES)).astype(BF16)


def get_counts(ref, columns):
    return ref[ref.shape[0] - TAIL :].astype(F32)[:1, :columns]


def by_column(values, anchor, columns):
    spot = lax.broadcasted_iota(jnp.int32, (columns, columns), 0) - anchor
    spot = jnp.where(spot < 0, spot + columns, spot)
    picked = spot == lax.broadcasted_iota(jnp.int32, (columns, columns), 1)
    return jnp.sum(jnp.where(picked, values, 0.0), axis=1, keepdims=True)


def first_kernel(size, rows, mix, mix_other, full, full_other, edges, w, table, gather, spread, out, frame, acc, hidden):
    core = lax.axis_index("rows")
    height, columns, outs = hidden.shape
    half_cols, channels = columns // 2, frame.shape[2]
    count = height * columns * size
    clear_edges(frame)
    summed = jnp.zeros((1, channels), F32)
    squares = jnp.zeros((1, channels), F32)
    for ref in (mix, mix_other, full, full_other):
        v = row_of(ref, 0, 1, rows * half_cols, channels).astype(F32)
        summed += jnp.sum(v, axis=0, keepdims=True)
        squares += jnp.sum(v * v, axis=0, keepdims=True)
    mean, scale = group_scale(summed, squares, count, gather, spread)
    scale = scale * (0.5 * table[0:1])

    def normed(row):
        local = local_row(core, row % rows, rows)
        for ref, col in ((mix, 0), (full, half_cols)) if row < rows else ((mix_other, 0), (full_other, half_cols)):
            v = row_of(ref, local, rows, half_cols, channels).astype(F32)
            frame[1 + row, col : col + half_cols] = silu_of_twice((v - mean) * scale).astype(BF16)

    for row in range(height):
        normed(row)
    nine_taps(frame, w, acc)
    bias = half_of(table[2:3], outs, core)
    summed = jnp.zeros((1, outs), F32)
    squares = jnp.zeros((1, outs), F32)
    for row in range(height):
        v = joined_taps(acc, row, columns, outs, edges) + bias
        hidden[row] = v
        summed += jnp.sum(v, axis=0, keepdims=True)
        squares += jnp.sum(v * v, axis=0, keepdims=True)
    mean, scale = group_scale(summed, squares, count, gather, spread)
    scale = scale * (0.5 * half_of(table[1:2], outs, core))
    for row in range(height):
        put(out, row, height, silu_of_twice((hidden[row] - mean) * scale).astype(BF16))


def near_channels(outs):
    return outs // 128 * 128


def near_kernel(own, w, edges, part, frame, acc):
    core = lax.axis_index("rows")
    height, columns, near = frame.shape[0] - 2, frame.shape[1], frame.shape[2]
    outs = part.shape[2]
    clear_edges(frame)
    for row in range(height):
        mine = get(own, row, height, columns, outs)
        frame[1 + row] = jnp.where(core == 0, mine[:, :near], mine[:, outs - near :])
    nine_taps(frame, w, acc, core * (2 * outs - near))
    for row in range(height):
        part[row] = joined_taps(acc, row, columns, outs, edges)


def second_kernel(anchor_ref, own, other, w, edges, near_part, counts, load, mix_same, mix_cross, full_same, full_cross, frame, acc):
    core = lax.axis_index("rows")
    odd = (lax.axis_index("blk") & 1) == 1
    height, columns = frame.shape[0] - 2, frame.shape[1]
    outs = near_part.shape[2]
    near = near_channels(outs)
    rows, half_cols = height // 2, columns // 2
    clear_edges(frame)
    for row in range(height):
        mine = get(own, row, height, columns, outs)
        theirs = get(other, height - 1 - row, height, columns, outs)
        frame[1 + row] = jnp.where(
            core == 0,
            jnp.concatenate([mine[:, near:], theirs], axis=1),
            jnp.concatenate([theirs, mine[:, : outs - near]], axis=1),
        )
    nine_taps(frame, w, acc, (1 - core) * near)
    own_row = jnp.where(odd, get_counts(load, columns), counts[...].astype(F32))
    part = jnp.broadcast_to(by_column(own_row, anchor_ref[0], columns), (columns, outs))
    for row in range(height):
        value = ((joined_taps(acc, row, columns, outs, edges) + near_part[row]) * part).astype(BF16)
        mix, full = (mix_same, full_same) if row < rows else (mix_cross, full_cross)
        spot = row if row < rows else height - 1 - row
        put(mix, spot, rows, value[:half_cols])
        put(full, spot, rows, value[half_cols:])
    for out in (mix_same, full_same):
        put_counts(out, own_row)


def last_kernel(anchor_ref, base, counts, load, mix_own, mix_core, mix_same, mix_cross, full_same, full_cross, out, done, sems):
    core = lax.axis_index("rows")
    odd = (lax.axis_index("blk") & 1) == 1
    anchor = anchor_ref[0]
    rows, cols, outs = base.shape[0], base.shape[1], base.shape[2] // 2
    late = lax.broadcasted_iota(jnp.int32, (cols, outs), 0) >= anchor
    keep = late ^ odd
    own_row = jnp.where(odd, get_counts(load, 2 * cols), counts[...].astype(F32))
    always = by_column(get_counts(full_same, 2 * cols), anchor, 2 * cols)[cols:]
    ours = by_column(own_row, anchor, 2 * cols)[:cols]
    theirs = by_column(get_counts(mix_same, 2 * cols), anchor, 2 * cols)[:cols]
    weight = always + jnp.where(keep[:, :1], ours, theirs)
    part = JOIN_SCALE / weight

    def summed(row, own, far, full):
        own, far, full = (get(ref, row, rows, cols, outs).astype(F32) for ref in (own, far, full))
        return jnp.where(keep, own, far) + full

    copies = []
    for row in range(rows):
        local = local_row(core, row, rows)
        same = summed(row, mix_own, mix_same, full_same)
        cross = summed(row, mix_core, mix_cross, full_cross)
        both = jnp.where(
            core == 0, jnp.concatenate([same, cross], axis=1), jnp.concatenate([cross, same], axis=1)
        )
        done[row] = base[row] + part * both
        copies.append(pltpu.make_async_copy(done.at[row], out.at[local], sems.at[row]))
        copies[row].start()
    for copy in copies:
        copy.wait()


def in_hbm(value):
    return pltpu.with_memory_space_constraint(value, pltpu.HBM)


def per_device(latent, offset, counts, conv_one, conv_two, gain_one, gain_two, time_bias):
    rows, stride, channels = latent.shape
    outs = conv_one.shape[3]
    size = channels // GROUPS
    height, columns = 2 * rows, 2 * stride
    odd = (lax.axis_index("blk") & 1) == 1
    anchor = offset[0]

    conv_one, conv_two = (jnp.swapaxes(v, 2, 3) for v in (conv_one, conv_two))
    lowered, load, held, counted = pl.pallas_call(
        lower_kernel,
        out_shape=(
            stacked(rows * stride, channels),
            stacked(rows * stride, channels, TAIL),
            jax.ShapeDtypeStruct(latent.shape, F32),
            jax.ShapeDtypeStruct(counts.shape, counts.dtype),
        ),
        in_specs=[HBM] * 2,
        out_specs=(VMEM,) * 4,
        scratch_shapes=[pltpu.SemaphoreType.DMA((rows + 1,))],
        compiler_params=PARAMS,
    )(in_hbm(latent), in_hbm(counts))
    weights = jax.ShapeDtypeStruct((3, 3 * outs, channels), BF16)
    vector = pltpu.VMEM((channels,), F32)
    w_first, w_next, table, gather, spread, base, edges = pl.pallas_call(
        functools.partial(ready_kernel, size),
        out_shape=(
            weights,
            weights,
            jax.ShapeDtypeStruct((8, channels), F32),
            jax.ShapeDtypeStruct((channels, 128), BF16),
            jax.ShapeDtypeStruct((128, channels), BF16),
            jax.ShapeDtypeStruct(latent.shape, F32),
            jax.ShapeDtypeStruct((2, columns, LANES), F32),
        ),
        in_specs=[SMEM, VMEM] + [HBM] * 5,
        out_specs=(VMEM,) * 7,
        scratch_shapes=[vector] * 3 + [pltpu.SemaphoreType.DMA((3,)), pltpu.SemaphoreType.DMA((2, 18))],
        compiler_params=PARAMS,
    )(offset, held, *[in_hbm(v) for v in (conv_one, conv_two, gain_one, gain_two, time_bias)])
    full = moved(lowered, lambda b: b ^ 1, 0)
    load = moved(load, lambda b: b + 2 if b % 2 else b - 2, 0)
    beyond = load[: lowered.shape[0]]
    blocks = (-1, stride, LANES)
    full_other = moved(full, lambda b: b, 1)
    lowered_blocks, beyond = lowered.reshape(blocks), beyond.reshape(blocks)
    col = lax.broadcasted_iota(jnp.int32, beyond.shape, 1)
    mix = jnp.where((col >= anchor) ^ odd, lowered_blocks, beyond).reshape(lowered.shape)
    mix_other = moved(mix, lambda b: b, 1)

    frame = pltpu.VMEM((height + 2, columns, channels), BF16)
    acc = pltpu.VMEM((height * columns, 3 * outs), F32)
    result = pltpu.VMEM((height, columns, outs), F32)
    own = pl.pallas_call(
        functools.partial(first_kernel, size, rows),
        out_shape=packed(height, columns, outs),
        in_specs=[VMEM] * 9,
        out_specs=VMEM,
        scratch_shapes=[frame, acc, result],
        compiler_params=PARAMS,
    )(mix, mix_other, full, full_other, edges, w_first, table, gather, spread)
    other = moved(own, lambda b: b, 1)
    near = near_channels(outs)
    near_part = pl.pallas_call(
        near_kernel,
        out_shape=jax.ShapeDtypeStruct((height, columns, outs), F32),
        in_specs=[VMEM] * 3,
        out_specs=VMEM,
        scratch_shapes=[pltpu.VMEM((height + 2, columns, near), BF16), acc],
        compiler_params=PARAMS,
    )(own, w_next, edges)
    marked, plain = packed(rows, stride, outs, TAIL), packed(rows, stride, outs)
    mix_same, mix_cross, full_same, full_cross = pl.pallas_call(
        second_kernel,
        out_shape=(marked, plain, marked, plain),
        in_specs=[SMEM] + [VMEM] * 7,
        out_specs=(VMEM,) * 4,
        scratch_shapes=[pltpu.VMEM((height + 2, columns, channels - near), BF16), acc],
        compiler_params=PARAMS,
    )(offset, own, other, w_next, edges, near_part, counted, load)

    def aside(b):
        return b - 2 if b % 2 else b + 2

    got_mix_same = moved(mix_same, aside, 0)
    got_mix_cross = moved(mix_cross, aside, 1)
    got_full_same = moved(full_same, lambda b: b ^ 1, 0)
    got_full_cross = moved(full_cross, lambda b: b ^ 1, 1)
    got_core = moved(mix_cross, lambda b: b, 1)
    return pl.pallas_call(
        last_kernel,
        out_shape=jax.ShapeDtypeStruct(latent.shape, F32),
        in_specs=[SMEM] + [VMEM] * 9,
        out_specs=HBM,
        scratch_shapes=[pltpu.VMEM(latent.shape, F32), pltpu.SemaphoreType.DMA((rows,))],
        compiler_params=PARAMS,
    )(offset, base, counted, load, mix_same, got_core, got_mix_same, got_mix_cross, got_full_same, got_full_cross)


def solution(mesh):
    return jax.shard_map(
        per_device,
        mesh=mesh,
        in_specs=(
            P(("pano", "rows"), "blk", None),
            P("pano"),
            P(("pano", "blk"), None),
            P(None, None, None, "rows"),
            P(None, None, None, "rows"),
            P(),
            P(),
            P(),
        ),
        out_specs=P(("pano", "rows"), "blk", None),
        check_vma=False,
    )
```
